32 devices in a mesh: el: 8 (over z, y), grp: 4 (over x, core).
Axes of the slice: x: 2, y: 2, z: 4, core: 2. Of those that a mesh axis runs over, the one named last changes fastest.
Arguments:
- conserved: float32 [16, 16, 64, 5, 512], P('el', 'grp'), as said below
- neighbours: int32 [16, 16, 64, 6], P('el', 'grp'), may hold values from -1 to 16383, as said below
- orientation: int32 [16, 16, 64], P('el', 'grp'), may hold values from 0 to 7
- coarse_block: int32 [16, 16, 64], P('el', 'grp'), may hold values from 0 to 511
Outputs:
- rate: float32 [16, 16, 64, 5, 512], P('el', 'grp')
- coarse_update: float32 [16, 16, 64, 5, 512], P('el', 'grp')
The draws below stay inside these ranges and needn't reach their ends.
Inputs may be any that keep to these rules, and one draw needn't show every extreme that they name: `conserved`: density and pressure at every node lie between 0.5 and 2. `neighbours`: a non-negative entry is the flat index (x 16 + y) * 64 + z of the element beside the face in the grid that is periodic in all three dimensions; walls lie only on faces of the first two directions and are seen from both sides.
All inputs are finite; a program needn't handle non-finite values.
Results may differ from the reference program's by a relative error of at most 0.0003.
Values sent between devices are 32-bit elements; how exact they have to be, the bound alone decides.
No kernel may reach another device: no remote copies, remote signals or barrier semaphores. Data moves between devices by JAX's collectives and lax.ppermute only.
A program may use at most 576 MiB of HBM per device.

```python
import math
import jax
import jax.numpy as jnp
import numpy as np
from jax import lax

NP = 8
BX = 2
ITERS = 4
EX = 16
EY = 16
EZ = 64
CB_GRP = 512
N_EL = 8


HEAT_RATIO = 1.4


def draw_conserved(key, part):
    grid_shape = (EX, EY, EZ, NP ** 3)
    subkeys = jax.random.split(jax.random.fold_in(key, 11), 3)
    density = jnp.exp(jax.random.uniform(subkeys[0], grid_shape, jnp.float32, math.log(0.5), math.log(2.0)))
    velocity = jnp.clip(0.3 * jax.random.normal(subkeys[1], (3,) + grid_shape, jnp.float32), -1.2, 1.2)
    pressure = jnp.exp(jax.random.uniform(subkeys[2], grid_shape, jnp.float32, math.log(0.5), math.log(2.0)))
    momentum = density[None] * velocity
    energy = pressure / (HEAT_RATIO - 1.0) + 0.5 * density * jnp.sum(velocity * velocity, axis=0)
    return jnp.stack([density, momentum[0], momentum[1], momentum[2], energy], axis=3).astype(jnp.float32)


def draw_neighbours(key, part):
    wall_bits = jax.random.randint(jax.random.fold_in(key, 23), (EX, EY, EZ, 2), 0, 4) == 0
    wall_bits = wall_bits.at[0, 0, 0, 0].set(True)
    index_x = lax.broadcasted_iota(jnp.int32, (EX, EY, EZ), 0)
    index_y = lax.broadcasted_iota(jnp.int32, (EX, EY, EZ), 1)
    index_z = lax.broadcasted_iota(jnp.int32, (EX, EY, EZ), 2)

    def flat_index(first_x, second_y, third_z):
        return (first_x % EX * EY + second_y % EY) * EZ + third_z % EZ
    wall_xm = jnp.roll(wall_bits[..., 0], 1, axis=0)
    wall_ym = jnp.roll(wall_bits[..., 1], 1, axis=1)
    entries = [jnp.where(wall_xm, -1, flat_index(index_x - 1, index_y, index_z)), jnp.where(wall_bits[..., 0], -1, flat_index(index_x + 1, index_y, index_z)), jnp.where(wall_ym, -1, flat_index(index_x, index_y - 1, index_z)), jnp.where(wall_bits[..., 1], -1, flat_index(index_x, index_y + 1, index_z)), flat_index(index_x, index_y, index_z - 1), flat_index(index_x, index_y, index_z + 1)]
    return jnp.stack(entries, axis=-1).astype(jnp.int32)


def touch_ends(values, key, least, largest):
    index_at = [jax.random.randint(jax.random.fold_in(key, axis), (), 0, length) for axis, length in enumerate(values.shape)]
    main_axis = values.shape.index(max(values.shape))
    next_to = index_at[:main_axis] + [(index_at[main_axis] + 1) % values.shape[main_axis]] + index_at[main_axis + 1:]
    return values.at[tuple(index_at)].set(least).at[tuple(next_to)].set(largest)


def setup_inputs(seed: int = 0) -> dict:
    keys = jax.random.split(jax.random.key(seed), 5)
    return {
        "conserved": draw_conserved(jax.random.fold_in(keys[4], 71), 0),
        "neighbours": draw_neighbours(jax.random.fold_in(keys[4], 71), 0),
        "orientation": touch_ends(jax.random.randint(keys[2], (EX, EY, EZ), 0, 8), jax.random.fold_in(keys[2], 1), 0, 7).astype(jnp.int32),
        "coarse_block": touch_ends(jax.random.randint(keys[3], (EX, EY, EZ), 0, CB_GRP), jax.random.fold_in(keys[3], 1), 0, CB_GRP - 1).astype(jnp.int32),
    }


HEAT_RATIO = 1.4
VISCOSITY = 0.02
TIME_STEP = 0.01
COARSE_SHIFT = 1.0
RELAX = 2.0 / 3.0
PRECISE = lax.Precision.HIGHEST

def legendre_rows(points, degree):
    rows = [points * 0.0 + 1.0, points.copy()]
    for order in range(1, degree):
        rows.append(((2 * order + 1) * points * rows[order] - order * rows[order - 1]) / (order + 1))
    return rows

def node_tables(npoints):
    degree = npoints - 1
    points = np.cos(np.pi * np.arange(npoints) / degree)
    for sweep_idx in range(100):
        values = legendre_rows(points, degree)
        previous = points
        points = previous - (previous * values[degree] - values[degree - 1]) / (npoints * values[degree])
    points = np.sort(points)
    legendre = legendre_rows(points, degree)[degree]
    weights = 2.0 / (degree * (degree + 1) * legendre ** 2)
    derivative = np.zeros((npoints, npoints))
    for row_idx in range(npoints):
        for col_idx in range(npoints):
            if row_idx != col_idx:
                derivative[row_idx, col_idx] = legendre[row_idx] / legendre[col_idx] / (points[row_idx] - points[col_idx])
    derivative[0, 0] = -degree * (degree + 1) / 4.0
    derivative[-1, -1] = degree * (degree + 1) / 4.0
    linear = np.stack([(1.0 - points) / 2.0, (1.0 + points) / 2.0], axis=1)
    return (weights, derivative, linear)

def coarse_operator():
    adjacency = np.zeros((8, 8))
    for row_idx in range(8):
        for bit_pos in range(3):
            adjacency[row_idx, row_idx ^ 1 << bit_pos] = 1.0
    return (COARSE_SHIFT + 3.0) * np.eye(8) - adjacency

def mirror_signs(direction):
    signs = np.ones((5, 1))
    signs[1 + direction, 0] = -1.0
    return jnp.asarray(signs, jnp.float32)

def contract(matrix, nodal, direction):
    patterns = ['ij,...jbc->...ibc', 'ij,...ajc->...aic', 'ij,...abj->...abi']
    return jnp.einsum(patterns[direction], matrix, nodal, precision=PRECISE)

def face_trace(nodal, direction, face_side):
    position = face_side * (nodal.shape[-1] - 1)
    if direction == 0:
        surface = nodal[..., position, :, :]
    elif direction == 1:
        surface = nodal[..., :, position, :]
    else:
        surface = nodal[..., :, :, position]
    return surface.reshape(surface.shape[:-2] + (surface.shape[-2] * surface.shape[-1],))

def add_plane(nodal, direction, position, values):
    extent = nodal.shape[-1]
    shaped = values.reshape(values.shape[:-1] + (extent, extent))
    if direction == 0:
        return nodal.at[..., position, :, :].add(shaped)
    if direction == 1:
        return nodal.at[..., :, position, :].add(shaped)
    return nodal.at[..., :, :, position].add(shaped)

def reorient(nodal, orientation):
    for direction in range(3):
        flagged = orientation // 2 ** direction % 2 == 1
        flipped = jnp.flip(nodal, axis=nodal.ndim - 3 + direction)
        nodal = jnp.where(flagged[..., None, None, None, None], flipped, nodal)
    return nodal

def euler_flux(fields_in, direction):
    density = fields_in[..., 0, :]
    momentum = fields_in[..., 1:4, :]
    energy = fields_in[..., 4, :]
    velocity = momentum / density[..., None, :]
    pressure = (HEAT_RATIO - 1.0) * (energy - 0.5 * lax.optimization_barrier(jnp.sum(momentum * velocity, axis=-2)))
    normal_vel = velocity[..., direction, :]
    unit_vec = jnp.asarray(np.eye(3)[:, direction:direction + 1], jnp.float32)
    flux_mom = momentum * normal_vel[..., None, :] + pressure[..., None, :] * unit_vec
    fluxes = jnp.concatenate([momentum[..., direction:direction + 1, :], flux_mom, (normal_vel * (energy + pressure))[..., None, :]], axis=-2)
    speeds = jnp.abs(normal_vel) + jnp.sqrt(HEAT_RATIO * pressure / density)
    return (fluxes, speeds)

def gradient_fields(natural, outside_u, weights, derivative):
    last_node = natural.shape[-1] - 1
    gradients = []
    for direction in range(3):
        gradient = contract(derivative, natural, direction)
        for face_side in range(2):
            normal_sign = 2.0 * face_side - 1.0
            position = face_side * last_node
            inside = face_trace(natural, direction, face_side)
            jump_term = normal_sign * 0.5 * (outside_u[2 * direction + face_side] - inside) / weights[position]
            gradient = add_plane(gradient, direction, position, jump_term)
        gradients.append(gradient)
    return gradients

def rate_of(natural, gradients, outside_u, outside_q, weights, derivative):
    last_node = natural.shape[-1] - 1
    leading = natural.shape[:-3]
    flattened = natural.reshape(leading + (natural.shape[-1] ** 3,))
    contribs = []
    for direction in range(3):
        fluxes, speeds = euler_flux(flattened, direction)
        contrib = contract(derivative, fluxes.reshape(natural.shape), direction) - VISCOSITY * contract(derivative, gradients[direction], direction)
        for face_side in range(2):
            normal_sign = 2.0 * face_side - 1.0
            position = face_side * last_node
            inside = face_trace(natural, direction, face_side)
            outside = outside_u[2 * direction + face_side]
            flux_in, speed_in = euler_flux(inside, direction)
            flux_out, speed_out = euler_flux(outside, direction)
            wave_speed = jnp.maximum(speed_in, speed_out)[..., None, :]
            jump_term = 0.5 * normal_sign * (flux_out - flux_in) - 0.5 * wave_speed * (outside - inside)
            viscous = 0.5 * normal_sign * (outside_q[2 * direction + face_side] - face_trace(gradients[direction], direction, face_side))
            contrib = add_plane(contrib, direction, position, (jump_term - VISCOSITY * viscous) / weights[position])
        contribs.append(contrib)
    return -(contribs[0] + contribs[1] + contribs[2])

def restrict(nodal, linear):
    coarse = nodal
    for direction in range(3):
        coarse = contract(linear.T, coarse, direction)
    return coarse

def prolong(coarse, linear):
    nodal = coarse
    for direction in range(3):
        nodal = contract(linear, nodal, direction)
    return nodal

def jacobi_sweeps(right_side, block_counts):
    blocks = right_side.reshape(-1, 5, 8)
    scaled = (block_counts + 1.0)[:, None, None]
    diagonal = scaled * (COARSE_SHIFT + 3.0)
    operator_mat = jnp.asarray(coarse_operator(), jnp.float32)
    coarse = jnp.zeros_like(blocks)
    for sweep_step in range(ITERS):
        applied = scaled * jnp.einsum('nfi,ij->nfj', coarse, operator_mat, precision=PRECISE)
        coarse = coarse + RELAX * (blocks - applied) / diagonal
    return coarse.reshape(-1, 40)

def outer_global(fields_list, neighbours, mirrored):
    results = []
    for direction in range(3):
        for face_side in range(2):
            inside = face_trace(fields_list[direction], direction, face_side)
            opposite = face_trace(fields_list[direction], direction, 1 - face_side)
            flattened = opposite.reshape((-1,) + opposite.shape[3:])
            column = neighbours[..., 2 * direction + face_side]
            fetched = jnp.take(flattened, jnp.maximum(column, 0).reshape(-1).astype(jnp.int32), axis=0).reshape(inside.shape)
            fallback = inside * mirror_signs(direction) if mirrored else inside
            results.append(jnp.where((column < 0)[..., None, None], fallback, fetched))
    return results

def reference(conserved, neighbours, orientation, coarse_block):
    weights_np, derivative_np, linear_np = node_tables(NP)
    weights = [float(value) for value in weights_np]
    derivative = jnp.asarray(derivative_np, jnp.float32)
    linear = jnp.asarray(linear_np, jnp.float32)
    grid_shape = conserved.shape[0:3]
    natural = reorient(conserved.reshape(grid_shape + (5, NP, NP, NP)), orientation)
    outside_u = outer_global([natural, natural, natural], neighbours, True)
    gradients = gradient_fields(natural, outside_u, weights, derivative)
    outside_q = outer_global(gradients, neighbours, False)
    rates = rate_of(natural, gradients, outside_u, outside_q, weights, derivative)
    rate = (TIME_STEP * reorient(rates, orientation)).reshape(grid_shape + (5, NP ** 3))
    slab_index = lax.broadcasted_iota(jnp.int32, grid_shape, 0) // BX
    global_block = (slab_index * CB_GRP + coarse_block).reshape(-1).astype(jnp.int32)
    restricted = restrict(rates, linear).reshape(-1, 40)
    block_total = N_EL * CB_GRP
    right_side = jax.ops.segment_sum(restricted, global_block, num_segments=block_total)
    block_counts = jax.ops.segment_sum(jnp.ones(global_block.shape, jnp.float32), global_block, num_segments=block_total)
    smoothed = jacobi_sweeps(right_side, block_counts)
    picked = jnp.take(smoothed, global_block, axis=0).reshape(grid_shape + (5, 2, 2, 2))
    correction = prolong(picked, linear)
    coarse_update = (TIME_STEP * reorient(correction, orientation)).reshape(grid_shape + (5, NP ** 3))
    return (rate, coarse_update)
```

```python
import functools
import jax
import jax.numpy as jnp
import numpy as np
from jax import lax
from jax.experimental import pallas as pl
from jax.experimental.pallas import tpu as pltpu
from jax.sharding import PartitionSpec as P

NP = 8
NODES = NP**3
FACE = 2 * NP * NP
ITERS = 4
FIELDS = 5
CORNERS = 8

HEAT_RATIO = 1.4
VISCOSITY = 0.02
TIME_STEP = 0.01
COARSE_SHIFT = 1.0
RELAX = 2.0 / 3.0

F32 = jnp.float32
BF16 = jnp.bfloat16
VMEM_BYTES = 56 * 1024 * 1024


def legendre_rows(points, degree):
    rows = [points * 0.0 + 1.0, points.copy()]
    for order in range(1, degree):
        rows.append(
            ((2 * order + 1) * points * rows[order] - order * rows[order - 1]) / (order + 1)
        )
    return rows


def node_tables(npoints):
    degree = npoints - 1
    points = np.cos(np.pi * np.arange(npoints) / degree)
    for sweep_idx in range(100):
        values = legendre_rows(points, degree)
        previous = points
        points = previous - (previous * values[degree] - values[degree - 1]) / (
            npoints * values[degree]
        )
    points = np.sort(points)
    legendre = legendre_rows(points, degree)[degree]
    weights = 2.0 / (degree * (degree + 1) * legendre**2)
    derivative = np.zeros((npoints, npoints))
    for row_idx in range(npoints):
        for col_idx in range(npoints):
            if row_idx != col_idx:
                derivative[row_idx, col_idx] = (
                    legendre[row_idx] / legendre[col_idx] / (points[row_idx] - points[col_idx])
                )
    derivative[0, 0] = -degree * (degree + 1) / 4.0
    derivative[-1, -1] = degree * (degree + 1) / 4.0
    linear = np.stack([(1.0 - points) / 2.0, (1.0 + points) / 2.0], axis=1)
    return (weights, derivative, linear)


def hi_lo(matrix):
    high = np.asarray(matrix, np.float32).astype(jnp.bfloat16)
    rest = np.asarray(matrix, np.float64) - high.astype(np.float64)
    return high, rest.astype(np.float32).astype(jnp.bfloat16)


@functools.lru_cache(maxsize=None)
def tables():
    weights, der, linear = node_tables(NP)
    w_end = weights[0]
    eye = np.eye(NP)
    full = [
        np.kron(np.kron(der, eye), eye),
        np.kron(np.kron(eye, der), eye),
        np.kron(np.kron(eye, eye), der),
    ]
    out = {"derivative": der, "w_end": w_end}
    lap = sum(mat @ mat for mat in full)
    dense = np.concatenate(
        [-TIME_STEP * full[0].T, TIME_STEP * VISCOSITY * lap.T], axis=0
    )
    out["dense"] = hi_lo(dense)
    half = NODES // 2
    out["planes"] = hi_lo(
        np.concatenate(
            [-TIME_STEP * full[1].T[:half, :half], -TIME_STEP * full[2].T[:half, :half]], axis=0
        )
    )
    node = np.arange(NODES)
    coords = [node // (NP * NP), node // NP % NP, node % NP]
    tangents = [(1, 2), (0, 2), (0, 1)]
    select, slope, lift_a, lift_b = [], [], [], []
    for direction in range(3):
        sel = np.zeros((NODES, FACE))
        own = np.zeros((FACE, NODES))
        ext = np.zeros((FACE, NODES))
        first, second = tangents[direction]
        for side in range(2):
            end = side * (NP - 1)
            lane = side * NP * NP + coords[first] * NP + coords[second]
            on_face = coords[direction] == end
            sel[node[on_face], lane[on_face]] = 1.0
            own[lane[on_face], node[on_face]] = -TIME_STEP / w_end
            ext[lane, node] = (
                TIME_STEP
                * VISCOSITY
                * (2 * side - 1)
                / (2.0 * w_end)
                * der[coords[direction], end]
            )
        select.append(sel)
        slope.append(full[direction].T @ sel)
        lift_a.append(own)
        lift_b.append(ext)
    out["trace_b"] = hi_lo(np.concatenate([select[1], slope[1]], axis=1))
    out["trace_c"] = hi_lo(np.concatenate([select[2], slope[2]], axis=1))
    out["lift"] = hi_lo(np.concatenate(lift_a + lift_b, axis=0))
    corner = np.zeros((NODES, CORNERS))
    for idx in range(CORNERS):
        corner[:, idx] = (
            linear[coords[0], idx // 4] * linear[coords[1], idx // 2 % 2] * linear[coords[2], idx % 2]
        )
    restrict = np.zeros((NODES, 128))
    restrict[:, :CORNERS] = corner / TIME_STEP
    out["restrict"] = hi_lo(restrict)
    adjacency = np.zeros((CORNERS, CORNERS))
    for idx in range(CORNERS):
        for bit in range(3):
            adjacency[idx, idx ^ (1 << bit)] = 1.0
    diagonal = COARSE_SHIFT + 3.0
    operator = diagonal * np.eye(CORNERS) - adjacency
    smooth = np.zeros((CORNERS, CORNERS))
    for sweep_idx in range(ITERS):
        smooth = smooth + RELAX * (np.eye(CORNERS) - operator @ smooth) / diagonal
    prolong = TIME_STEP * corner @ smooth
    width = FIELDS * CORNERS
    spread = np.zeros((width, FIELDS * NODES))
    for field in range(FIELDS):
        spread[
            field * CORNERS : (field + 1) * CORNERS, field * NODES : (field + 1) * NODES
        ] = prolong.T
    spread_hi, spread_lo = hi_lo(spread)
    out["spread"] = np.concatenate(
        [spread_hi, spread_hi, spread_lo, np.zeros((128 - 3 * width, FIELDS * NODES), spread_hi.dtype)],
        axis=0,
    )
    return out


def split(value):
    high = value.astype(BF16)
    return high, (value - high.astype(F32)).astype(BF16)


def dot3(lhs_hi, lhs_lo, rhs_hi, rhs_lo):
    return (
        jnp.dot(lhs_hi, rhs_hi, preferred_element_type=F32)
        + jnp.dot(lhs_lo, rhs_hi, preferred_element_type=F32)
        + jnp.dot(lhs_hi, rhs_lo, preferred_element_type=F32)
    )


def lanes_of(shape):
    return lax.broadcasted_iota(jnp.int32, shape, len(shape) - 1)


def bit_of(code, position):
    return lax.shift_right_logical(code, position) & 1


def face_index(code, direction):
    bits = [bit_of(code, axis) for axis in range(3)]
    others = [axis for axis in range(3) if axis != direction]
    mask = bits[direction] * 64 + bits[others[0]] * 56 + bits[others[1]] * 7
    return lanes_of(code.shape) ^ mask


def sign_of(code, direction):
    return (1 - 2 * bit_of(code, direction)).astype(F32)


def permute(value, index):
    return jnp.take_along_axis(value, index, axis=1)


def swap_sides(value):
    return pltpu.roll(value, FACE // 2, 1)


def pack_sides(state, slope):
    lower = lanes_of(state.shape) < FACE // 2
    turned = swap_sides(slope)
    return jnp.where(lower, state, turned), jnp.where(lower, turned, state)


def trace_kernel(last_x, last_y, der, x_ref, code_ref, bhi_ref, blo_ref, pa_ref, pb_ref, xm_ref, xp_ref, ym_ref, yp_ref):
    rows = x_ref.shape[3]
    place_x, place_y = pl.program_id(0), pl.program_id(1)
    code = code_ref[0, 0]
    lower = lanes_of((rows, FACE)) < FACE // 2
    index_a = face_index(code, 0)
    sign_a = sign_of(code, 0)
    index_b = face_index(code, 1)
    sign_b = sign_of(code, 1)
    stacked = x_ref[0, 0].reshape(FIELDS * rows, NODES)
    high, low = split(stacked)
    along_b = dot3(high, low, bhi_ref[...], blo_ref[...])
    straight = [
        jnp.where(lower, float(der[0, 2 * tile]), float(der[NP - 1, 2 * tile + 1]))
        for tile in range(4)
    ]
    crossed = [
        jnp.where(lower, float(der[0, 2 * tile + 1]), float(der[NP - 1, 2 * tile]))
        for tile in range(4)
    ]
    for field in range(FIELDS):
        parts = [x_ref[0, 0, field, :, FACE * tile : FACE * (tile + 1)] for tile in range(4)]
        state = jnp.where(lower, parts[0], parts[3])
        plain = parts[0] * straight[0]
        other = parts[0] * crossed[0]
        for tile in range(1, 4):
            plain = plain + parts[tile] * straight[tile]
        turned = [swap_sides(part) for part in parts]
        other = turned[0] * crossed[0]
        for tile in range(1, 4):
            other = other + turned[tile] * crossed[tile]
        slope = plain + other
        minus, plus = pack_sides(permute(state, index_a), sign_a * permute(slope, index_a))
        pa_ref[0, 0, 0, field] = minus
        pa_ref[0, 0, 1, field] = plus
        rows_f = slice(field * rows, (field + 1) * rows)
        minus, plus = pack_sides(
            permute(along_b[rows_f, :FACE], index_b),
            sign_b * permute(along_b[rows_f, FACE:], index_b),
        )
        pb_ref[0, 0, 0, field] = minus
        pb_ref[0, 0, 1, field] = plus

    @pl.when(place_x == 0)
    def _():
        xm_ref[0] = pa_ref[0, 0, 0]

    @pl.when(place_x == last_x)
    def _():
        xp_ref[0] = pa_ref[0, 0, 1]

    @pl.when(place_y == 0)
    def _():
        ym_ref[0] = pb_ref[0, 0, 0]

    @pl.when(place_y == last_y)
    def _():
        yp_ref[0] = pb_ref[0, 0, 1]


def volume_kernel(x_ref, code_ref, dhi_ref, dlo_ref, phi_ref, plo_ref, chi_ref, clo_ref, v_ref, pc_ref, hi_ref, lo_ref):
    pair = x_ref.shape[1]
    rows = x_ref.shape[3]
    chunk = 16
    steps = rows // chunk
    total = pair * rows

    def body(step, carry):
        for half in range(pair):
            start = pl.multiple_of(step * chunk, chunk)
            code = code_ref[0, half, pl.ds(start, chunk), :]
            signs = [sign_of(code, axis) for axis in range(3)]
            for tile in range(4):
                lanes = slice(FACE * tile, FACE * (tile + 1))
                fields = [x_ref[0, half, field, pl.ds(start, chunk), lanes] for field in range(FIELDS)]
                density, energy = fields[0], fields[4]
                momentum = fields[1:4]
                inverse = 1.0 / density
                kinetic = (
                    momentum[0] * momentum[0] + momentum[1] * momentum[1] + momentum[2] * momentum[2]
                ) * inverse
                pressure = (HEAT_RATIO - 1.0) * (energy - 0.5 * kinetic)
                enthalpy = energy + pressure

                def put(field, slot, value):
                    first = field * total + half * rows
                    where_rows = pl.ds(pl.multiple_of(first + start, chunk), chunk)
                    where_lanes = slice(NODES * slot + FACE * tile, NODES * slot + FACE * (tile + 1))
                    high, low = split(value)
                    hi_ref[where_rows, where_lanes] = high
                    lo_ref[where_rows, where_lanes] = low

                for field in range(FIELDS):
                    put(field, 1, fields[field])
                for axis, slot in ((0, 0), (1, 2), (2, 3)):
                    mass = momentum[axis] * signs[axis]
                    speed = mass * inverse
                    put(0, slot, mass)
                    for part in range(3):
                        flux = momentum[part] * speed
                        if part == axis:
                            flux = flux + pressure * signs[axis]
                        put(1 + part, slot, flux)
                    put(4, slot, enthalpy * speed)
        return carry

    lax.fori_loop(0, steps, body, 0)
    half_nodes = NODES // 2
    for side in range(2):
        cols = slice(half_nodes * side, half_nodes * (side + 1))
        acc = dot3(hi_ref[:, : 2 * NODES], lo_ref[:, : 2 * NODES], dhi_ref[:, cols], dlo_ref[:, cols])
        for part in range(2):
            first = NODES * (2 + part) + half_nodes * side
            lanes = slice(first, first + half_nodes)
            block = slice(half_nodes * part, half_nodes * (part + 1))
            acc = acc + dot3(hi_ref[:, lanes], lo_ref[:, lanes], phi_ref[block, :], plo_ref[block, :])
        for half in range(pair):
            for field in range(FIELDS):
                first = field * total + half * rows
                v_ref[0, half, field, :, cols] = acc[first : first + rows, :]
    along_c = dot3(hi_ref[:, NODES : 2 * NODES], lo_ref[:, NODES : 2 * NODES], chi_ref[...], clo_ref[...])
    for half in range(pair):
        code = code_ref[0, half]
        index_c = face_index(code, 2)
        sign_c = sign_of(code, 2)
        for field in range(FIELDS):
            first = field * total + half * rows
            pc_ref[0, half, 0, field] = permute(along_c[first : first + rows, :FACE], index_c)
            pc_ref[0, half, 1, field] = sign_c * permute(along_c[first : first + rows, FACE:], index_c)


def normal_flux(state, axis):
    density, energy = state[0], state[4]
    momentum = state[1:4]
    inverse = 1.0 / density
    kinetic = (
        momentum[0] * momentum[0] + momentum[1] * momentum[1] + momentum[2] * momentum[2]
    ) * inverse
    pressure = (HEAT_RATIO - 1.0) * (energy - 0.5 * kinetic)
    speed = momentum[axis] * inverse
    flux = [momentum[axis]]
    for part in range(3):
        value = momentum[part] * speed
        flux.append(value + pressure if part == axis else value)
    flux.append(speed * (energy + pressure))
    return flux, jnp.abs(speed) + jnp.sqrt(HEAT_RATIO * pressure * inverse)


def face_kernel(
    last_x, last_y, v_ref, code_ref, block_ref, pa_ref, al_ref, ar_ref, hxl_ref, hxr_ref,
    pb_ref, bl_ref, br_ref, hyl_ref, hyr_ref, pc_ref, lhi_ref, llo_ref, rhi_ref, rlo_ref,
    rate_ref, sums_ref, hi_ref, lo_ref, coarse_ref,
):
    rows = v_ref.shape[3]
    place_x, place_y = pl.program_id(0), pl.program_id(1)
    chunk = 16

    def body(step, carry):
        start = pl.multiple_of(step * chunk, chunk)
        here = pl.ds(start, chunk)
        code = code_ref[0, 0, here, :]
        lane = lanes_of((chunk, FACE))
        lower = lane < FACE // 2
        outward = jnp.where(lower, -1.0, 1.0)
        for axis in range(2):
            own_ref = (pa_ref, pb_ref)[axis]
            left_ref = (al_ref, bl_ref)[axis]
            right_ref = (ar_ref, br_ref)[axis]
            left_halo = (hxl_ref, hyl_ref)[axis]
            right_halo = (hxr_ref, hyr_ref)[axis]
            at_first = ((place_x, place_y)[axis] == 0)
            at_last = ((place_x, place_y)[axis] == (last_x, last_y)[axis])
            wall = bit_of(code, 3 + 2 * axis)
            wall = jnp.where(lower, wall, bit_of(code, 4 + 2 * axis)) == 1
            inside, outside, slopes = [], [], []
            for field in range(FIELDS):
                minus = own_ref[0, 0, 0, field, here, :]
                plus = own_ref[0, 0, 1, field, here, :]
                left = jnp.where(at_first, left_halo[0, field, here, :], left_ref[0, 0, 0, field, here, :])
                right = jnp.where(at_last, right_halo[0, field, here, :], right_ref[0, 0, 0, field, here, :])
                state = jnp.where(lower, minus, plus)
                slope = swap_sides(jnp.where(lower, plus, minus))
                far = swap_sides(jnp.where(lower, right, left))
                far_slope = jnp.where(lower, left, right)
                mirror = -state if field == 1 + axis else state
                inside.append(state)
                outside.append(jnp.where(wall, mirror, far))
                slopes.append(jnp.where(wall, 0.0, far_slope - slope))
            finish(axis, start, code, inside, outside, slopes, outward)
        return carry

    def finish(axis, start, code, inside, outside, slopes, outward):
        index = face_index(code, axis)
        flux_in, speed_in = normal_flux(inside, axis)
        flux_out, speed_out = normal_flux(outside, axis)
        wave = 0.5 * jnp.maximum(speed_in, speed_out)
        half_out = 0.5 * outward
        for field in range(FIELDS):
            jump = outside[field] - inside[field]
            total = (
                half_out * (flux_out[field] - flux_in[field] - VISCOSITY * slopes[field]) - wave * jump
            )
            where_rows = pl.ds(pl.multiple_of(field * rows + start, chunk), chunk)
            for slot, value in ((axis, total), (3 + axis, jump)):
                high, low = split(permute(value, index))
                hi_ref[where_rows, FACE * slot : FACE * (slot + 1)] = high
                lo_ref[where_rows, FACE * slot : FACE * (slot + 1)] = low

    lax.fori_loop(0, rows // chunk, body, 0)

    code = code_ref[0, 0]
    lower = lanes_of((rows, FACE)) < FACE // 2
    far_all, slope_all = [], []
    for field in range(FIELDS):
        for kind, store in ((0, far_all), (1, slope_all)):
            value = pc_ref[0, 0, kind, field]
            ahead = pltpu.roll(value, rows - 1, 0)
            behind = pltpu.roll(value, 1, 0)
            store.append(swap_sides(jnp.where(lower, ahead, behind)))
    for step in range(rows // chunk):
        here = slice(step * chunk, (step + 1) * chunk)
        outward = jnp.where(lower[here], -1.0, 1.0)
        inside = [pc_ref[0, 0, 0, field, here, :] for field in range(FIELDS)]
        outside = [far_all[field][here] for field in range(FIELDS)]
        slopes = [slope_all[field][here] - pc_ref[0, 0, 1, field, here, :] for field in range(FIELDS)]
        finish(2, step * chunk, code[here], inside, outside, slopes, outward)

    change = dot3(hi_ref[...], lo_ref[...], lhi_ref[...], llo_ref[...])
    rate = v_ref[0, 0].reshape(FIELDS * rows, NODES) + change
    rate_ref[0, 0] = rate.reshape(FIELDS, rows, NODES)
    high, low = split(rate)
    coarse = dot3(high, low, rhi_ref[...], rlo_ref[...])
    packed = coarse[:rows]
    for field in range(1, FIELDS):
        packed = packed + pltpu.roll(coarse[field * rows : (field + 1) * rows], CORNERS * field, 1)
    lane = lanes_of((rows, 128))
    corner = bit_of(code, 0) * 4 + bit_of(code, 1) * 2 + bit_of(code, 2)
    packed = permute(packed, lane ^ corner)
    packed = jnp.where(lane == FIELDS * CORNERS, 1.0, packed)
    place = place_x * (last_y + 1) + place_y
    coarse_ref[pl.ds(pl.multiple_of(place * rows, rows), rows), :] = packed

    @pl.when((place_x == last_x) & (place_y == last_y))
    def _():
        height = sums_ref.shape[0]
        count = sums_ref.shape[1]
        turned = coarse_ref[...].T[:height]
        first, second = split(turned)
        block = block_ref[...]
        slots = lax.broadcasted_iota(jnp.int32, (block.shape[0], count), 1)
        wide = jnp.concatenate([block] * (count // 128), axis=1)
        onehot = jnp.where(wide == slots, 1.0, 0.0).astype(BF16)
        sums_ref[...] = jnp.dot(first, onehot, preferred_element_type=F32) + jnp.dot(
            second, onehot, preferred_element_type=F32
        )


def prolong_kernel(sums_ref, more_ref, code_ref, block_ref, spread_ref, out_ref, table_ref):
    rows = out_ref.shape[3]
    count = sums_ref.shape[1]
    width = FIELDS * CORNERS

    @pl.when((pl.program_id(0) == 0) & (pl.program_id(1) == 0))
    def _():
        total = sums_ref[...] + more_ref[...]
        scaled = total[:width] / (total[width : width + 1] + 1.0)
        high = scaled.astype(BF16).astype(F32)
        low = scaled - high
        pad = jnp.zeros((128 - 3 * width, count), F32)
        table_ref[...] = jnp.concatenate([high, low, high, pad], axis=0).astype(BF16)

    code = code_ref[0, 0]
    block = block_ref[0, 0]
    slots = lax.broadcasted_iota(jnp.int32, (rows, count), 1)
    wide = jnp.concatenate([block] * (count // 128), axis=1)
    onehot = jnp.where(wide == slots, 1.0, 0.0).astype(BF16)
    picked = lax.dot_general(
        onehot, table_ref[...], (((1,), (1,)), ((), ())), preferred_element_type=F32
    )
    corner = bit_of(code, 0) * 4 + bit_of(code, 1) * 2 + bit_of(code, 2)
    picked = permute(picked, lanes_of((rows, 128)) ^ corner).astype(BF16)
    for field in range(FIELDS):
        lanes = slice(NODES * field, NODES * (field + 1))
        out_ref[0, 0, field] = jnp.dot(picked, spread_ref[:, lanes], preferred_element_type=F32)


def whole(array):
    dims = array.ndim
    return pl.BlockSpec(array.shape, lambda *_: (0,) * dims, pipeline_mode=pl.Buffered(1))


def params(dims):
    return pltpu.CompilerParams(
        dimension_semantics=("arbitrary",) * dims, vmem_limit_bytes=VMEM_BYTES
    )


def shift(value, axis, step):
    count = lax.axis_size(axis)
    return lax.ppermute(value, axis, [(i, (i + step) % count) for i in range(count)])


def per_device(conserved, neighbours, orientation, coarse_block):
    data = tables()
    der = data["derivative"]
    cx, cy, cz = conserved.shape[:3]
    last_x, last_y = cx - 1, cy - 1
    state = jnp.transpose(conserved, (0, 1, 3, 2, 4))
    code = orientation
    for face in range(6):
        code = code + jnp.where(neighbours[..., face] < 0, 1 << (3 + face), 0)
    code = jnp.broadcast_to(code[..., None], (cx, cy, cz, 128))
    blocks = jnp.broadcast_to(coarse_block[..., None], (cx, cy, cz, 128))
    count = lax.axis_size("grp") * (cx * cy * cz // 4)
    height = 48

    def state_spec(step):
        return pl.BlockSpec((1, step, FIELDS, cz, NODES), lambda x, y: (x, y, 0, 0, 0))

    def code_spec(step):
        return pl.BlockSpec((1, step, cz, 128), lambda x, y: (x, y, 0, 0))

    def pack_spec(step):
        return pl.BlockSpec((1, step, 2, FIELDS, cz, FACE), lambda x, y: (x, y, 0, 0, 0, 0))

    edge = (1, FIELDS, cz, FACE)
    pack_shape = jax.ShapeDtypeStruct((cx, cy, 2, FIELDS, cz, FACE), F32)
    bhi, blo = [jnp.asarray(m) for m in data["trace_b"]]
    pa, pb, xm, xp, ym, yp = pl.pallas_call(
        functools.partial(trace_kernel, last_x, last_y, der),
        grid=(cx, cy),
        in_specs=[state_spec(1), code_spec(1), whole(bhi), whole(blo)],
        out_specs=[
            pack_spec(1),
            pack_spec(1),
            pl.BlockSpec(edge, lambda x, y: (jnp.where(x == 0, y, last_y), 0, 0, 0)),
            pl.BlockSpec(edge, lambda x, y: (jnp.where(x == last_x, y, 0), 0, 0, 0)),
            pl.BlockSpec(edge, lambda x, y: (x, 0, 0, 0)),
            pl.BlockSpec(edge, lambda x, y: (x, 0, 0, 0)),
        ],
        out_shape=[
            pack_shape,
            pack_shape,
            jax.ShapeDtypeStruct((cy, FIELDS, cz, FACE), F32),
            jax.ShapeDtypeStruct((cy, FIELDS, cz, FACE), F32),
            jax.ShapeDtypeStruct((cx, FIELDS, cz, FACE), F32),
            jax.ShapeDtypeStruct((cx, FIELDS, cz, FACE), F32),
        ],
        compiler_params=params(2),
        name="traces",
    )(state, code, bhi, blo)
    from_left = shift(xp, "el", 1)
    from_right = shift(xm, "el", -1)
    from_below = shift(yp, "grp", 1)
    from_above = shift(ym, "grp", -1)

    pair = 2 if cy % 2 == 0 else 1
    dhi, dlo = [jnp.asarray(m) for m in data["dense"]]
    phi, plo = [jnp.asarray(m) for m in data["planes"]]
    chi, clo = [jnp.asarray(m) for m in data["trace_c"]]
    volume, pc = pl.pallas_call(
        volume_kernel,
        grid=(cx, cy // pair),
        in_specs=[state_spec(pair), code_spec(pair)] + [whole(m) for m in (dhi, dlo, phi, plo, chi, clo)],
        out_specs=[state_spec(pair), pack_spec(pair)],
        out_shape=[jax.ShapeDtypeStruct((cx, cy, FIELDS, cz, NODES), F32), pack_shape],
        scratch_shapes=[
            pltpu.VMEM((FIELDS * pair * cz, 4 * NODES), BF16),
            pltpu.VMEM((FIELDS * pair * cz, 4 * NODES), BF16),
        ],
        compiler_params=params(2),
        name="volume",
    )(state, code, dhi, dlo, phi, plo, chi, clo)

    side = (1, 1, 1, FIELDS, cz, FACE)
    lhi, llo = [jnp.asarray(m) for m in data["lift"]]
    rhi, rlo = [jnp.asarray(m) for m in data["restrict"]]
    flat_blocks = blocks.reshape(cx * cy * cz, 128)
    rate, sums = pl.pallas_call(
        functools.partial(face_kernel, last_x, last_y),
        grid=(cx, cy),
        in_specs=[
            state_spec(1),
            code_spec(1),
            whole(flat_blocks),
            pack_spec(1),
            pl.BlockSpec(side, lambda x, y: (jnp.maximum(x - 1, 0), y, 1, 0, 0, 0)),
            pl.BlockSpec(side, lambda x, y: (jnp.minimum(x + 1, last_x), y, 0, 0, 0, 0)),
            pl.BlockSpec(edge, lambda x, y: (y, 0, 0, 0)),
            pl.BlockSpec(edge, lambda x, y: (y, 0, 0, 0)),
            pack_spec(1),
            pl.BlockSpec(side, lambda x, y: (x, jnp.maximum(y - 1, 0), 1, 0, 0, 0)),
            pl.BlockSpec(side, lambda x, y: (x, jnp.minimum(y + 1, last_y), 0, 0, 0, 0)),
            pl.BlockSpec(edge, lambda x, y: (x, 0, 0, 0)),
            pl.BlockSpec(edge, lambda x, y: (x, 0, 0, 0)),
            pack_spec(1),
            whole(lhi),
            whole(llo),
            whole(rhi),
            whole(rlo),
        ],
        out_specs=[state_spec(1), pl.BlockSpec((height, count), lambda x, y: (0, 0))],
        out_shape=[
            jax.ShapeDtypeStruct((cx, cy, FIELDS, cz, NODES), F32),
            jax.ShapeDtypeStruct((height, count), F32),
        ],
        scratch_shapes=[
            pltpu.VMEM((FIELDS * cz, 6 * FACE), BF16),
            pltpu.VMEM((FIELDS * cz, 6 * FACE), BF16),
            pltpu.VMEM((cx * cy * cz, 128), F32),
        ],
        compiler_params=params(2),
        name="faces",
    )(
        volume, code, flat_blocks, pa, pa, pa, from_left, from_right, pb, pb, pb,
        from_below, from_above, pc, lhi, llo, rhi, rlo,
    )

    size = lax.axis_size("grp")
    more = jnp.zeros_like(sums)
    if size & (size - 1) == 0:
        stride = 1
        while stride < size:
            if stride > 1:
                sums = sums + more
            more = lax.ppermute(sums, "grp", [(i, i ^ stride) for i in range(size)])
            stride *= 2
    else:
        sums = lax.psum(sums, "grp")

    spread = jnp.asarray(data["spread"])
    update = pl.pallas_call(
        prolong_kernel,
        grid=(cx, cy),
        in_specs=[whole(sums), whole(more), code_spec(1), code_spec(1), whole(spread)],
        out_specs=state_spec(1),
        out_shape=jax.ShapeDtypeStruct((cx, cy, FIELDS, cz, NODES), F32),
        scratch_shapes=[pltpu.VMEM((128, count), BF16)],
        compiler_params=params(2),
        name="prolong",
    )(sums, more, code, blocks, spread)
    back = (0, 1, 3, 2, 4)
    return (jnp.transpose(rate, back), jnp.transpose(update, back))


def solution(mesh):
    in_specs = (
        P("el", "grp", None, None, None),
        P("el", "grp", None, None),
        P("el", "grp", None),
        P("el", "grp", None),
    )
    out_specs = (P("el", "grp", None, None, None), P("el", "grp", None, None, None))
    return jax.shard_map(
        per_device, mesh=mesh, in_specs=in_specs, out_specs=out_specs, check_vma=False
    )
```

```python
import functools
import jax
import jax.numpy as jnp
import numpy as np
from jax import lax
from jax.experimental import pallas as pl
from jax.experimental.pallas import tpu as pltpu
from jax.sharding import PartitionSpec as P

NP = 8
NODES = NP**3
FACE = 2 * NP * NP
ITERS = 4
FIELDS = 5
CORNERS = 8

HEAT_RATIO = 1.4
VISCOSITY = 0.02
TIME_STEP = 0.01
COARSE_SHIFT = 1.0
RELAX = 2.0 / 3.0

F32 = jnp.float32
BF16 = jnp.bfloat16
VMEM_BYTES = 58 * 1024 * 1024
VOLUME_STEP = 4
FACE_STEP = 2
TRACE_STEP = 2


def legendre_rows(points, degree):
    rows = [points * 0.0 + 1.0, points.copy()]
    for order in range(1, degree):
        rows.append(
            ((2 * order + 1) * points * rows[order] - order * rows[order - 1]) / (order + 1)
        )
    return rows


def node_tables(npoints):
    degree = npoints - 1
    points = np.cos(np.pi * np.arange(npoints) / degree)
    for sweep_idx in range(100):
        values = legendre_rows(points, degree)
        previous = points
        points = previous - (previous * values[degree] - values[degree - 1]) / (
            npoints * values[degree]
        )
    points = np.sort(points)
    legendre = legendre_rows(points, degree)[degree]
    weights = 2.0 / (degree * (degree + 1) * legendre**2)
    derivative = np.zeros((npoints, npoints))
    for row_idx in range(npoints):
        for col_idx in range(npoints):
            if row_idx != col_idx:
                derivative[row_idx, col_idx] = (
                    legendre[row_idx] / legendre[col_idx] / (points[row_idx] - points[col_idx])
                )
    derivative[0, 0] = -degree * (degree + 1) / 4.0
    derivative[-1, -1] = degree * (degree + 1) / 4.0
    linear = np.stack([(1.0 - points) / 2.0, (1.0 + points) / 2.0], axis=1)
    return (weights, derivative, linear)


def hi_lo(matrix):
    high = np.asarray(matrix, np.float32).astype(jnp.bfloat16)
    rest = np.asarray(matrix, np.float64) - high.astype(np.float64)
    return high, rest.astype(np.float32).astype(jnp.bfloat16)


@functools.lru_cache(maxsize=None)
def tables():
    weights, der, linear = node_tables(NP)
    w_end = weights[0]
    eye = np.eye(NP)
    full = [
        np.kron(np.kron(der, eye), eye),
        np.kron(np.kron(eye, der), eye),
        np.kron(np.kron(eye, eye), der),
    ]
    out = {"w_end": w_end, "derivative": der}
    lap = sum(mat @ mat for mat in full)
    half = NODES // 2
    mirror = np.arange(NODES).reshape(NP, NP * NP)[::-1].reshape(-1)
    lap = TIME_STEP * VISCOSITY * lap
    lap_even = 0.5 * (lap[:half, :half] + lap[:half, mirror[:half]])
    lap_odd = 0.5 * (lap[:half, :half] - lap[:half, mirror[:half]])
    flows = [-0.5 * TIME_STEP * full[axis].T[:half, :half] for axis in (1, 2)]
    out["planes"] = hi_lo(np.concatenate([lap_even.T, lap_odd.T] + flows, axis=0))
    node = np.arange(half)
    coords = [node // (NP * NP), node // NP % NP, node % NP]
    traces, lifts = [], []
    for half_idx in range(2):
        blocks, lift_rows = [], []
        for direction in (1, 2):
            other = coords[3 - direction]
            sel = np.zeros((half, FACE // 2))
            own = np.zeros((FACE // 2, half))
            ext = np.zeros((FACE // 2, half))
            for side in range(2):
                end = side * (NP - 1)
                lane = side * 32 + coords[0] * NP + other
                on_face = coords[direction] == end
                sel[node[on_face], lane[on_face]] = 1.0
                own[lane[on_face], node[on_face]] = -TIME_STEP / w_end
                ext[lane, node] = (
                    TIME_STEP * VISCOSITY * (2 * side - 1) / (2.0 * w_end) * der[coords[direction], end]
                )
            slope = full[direction].T[:half, :half] @ sel
            blocks += [sel, slope] if half_idx == direction - 1 else [slope, sel]
            lift_rows.append((own, ext))
        traces.append(np.concatenate(blocks, axis=1))
        if half_idx == 1:
            lift_rows = lift_rows[::-1]
        lifts.append(
            np.concatenate([row[0] for row in lift_rows] + [row[1] for row in lift_rows], axis=0)
        )
    out["traces"] = hi_lo(np.concatenate(traces, axis=0))
    out["lifts"] = hi_lo(np.concatenate(lifts, axis=0))
    lane = np.arange(FACE)
    upper = lane // (FACE // 2)
    pos_b, pos_c = lane // NP % NP, lane % NP
    restrict = np.zeros((2 * FACE, 128))
    for idx in range(CORNERS):
        weight = 0.5 / TIME_STEP * linear[pos_b, idx // 2 % 2] * linear[pos_c, idx % 2]
        restrict[:FACE, idx] = weight
        restrict[FACE:, idx] = weight * (2 * (idx // 4) - 1)
    out["restrict"] = hi_lo(restrict)
    place = linear[:, 1] - linear[:, 0]
    planes = [np.where(upper == 1, second, first) for first, second in PLANE_ORDER]
    rows = [place[plane] for plane in planes]
    flow = -TIME_STEP * der
    even = 0.5 * (flow[:4, :4] + flow[:4, :3:-1])
    odd = 0.5 * (flow[:4, :4] - flow[:4, :3:-1])
    mix = []
    for part in (even, odd):
        for first in range(2):
            for second in range(2):
                mix.append(part[2 * first + upper, 2 * second + upper])
                mix.append(part[2 * first + upper, 2 * second + 1 - upper])
    ends = (NP - 1) * upper
    slope_plain = [der[ends, plane] for plane in planes]
    slope_cross = [der[NP - 1 - ends, plane] for plane in planes]
    scale = TIME_STEP * VISCOSITY / (2.0 * w_end)
    lift_plain = [scale * (2 * upper - 1) * der[plane, ends] for plane in planes]
    lift_cross = [scale * (1 - 2 * upper) * der[plane, NP - 1 - ends] for plane in planes]
    out["lanes"] = {
        "mix": mix,
        "slope": slope_plain + slope_cross,
        "lift": lift_plain + lift_cross + rows,
    }
    adjacency = np.zeros((CORNERS, CORNERS))
    for idx in range(CORNERS):
        for bit in range(3):
            adjacency[idx, idx ^ (1 << bit)] = 1.0
    diagonal = COARSE_SHIFT + 3.0
    operator = diagonal * np.eye(CORNERS) - adjacency
    smooth = np.zeros((CORNERS, CORNERS))
    for sweep_idx in range(ITERS):
        smooth = smooth + RELAX * (np.eye(CORNERS) - operator @ smooth) / diagonal
    node = np.arange(NODES)
    coords = [node // (NP * NP), node // NP % NP, node % NP]
    corner = np.zeros((NODES, CORNERS))
    for idx in range(CORNERS):
        corner[:, idx] = (
            linear[coords[0], idx // 4] * linear[coords[1], idx // 2 % 2] * linear[coords[2], idx % 2]
        )
    prolong = TIME_STEP * corner @ smooth
    width = FIELDS * CORNERS
    spread = np.zeros((width, FIELDS * NODES))
    for field in range(FIELDS):
        spread[
            field * CORNERS : (field + 1) * CORNERS, field * NODES : (field + 1) * NODES
        ] = prolong.T
    spread_hi, spread_lo = hi_lo(spread)
    out["spread"] = np.concatenate(
        [spread_hi, spread_hi, spread_lo, np.zeros((128 - 3 * width, FIELDS * NODES), spread_hi.dtype)],
        axis=0,
    )
    return out


def lane_rows(rows, height):
    return np.stack([np.broadcast_to(row, (height, FACE)) for row in rows]).astype(np.float32)


def split(value):
    high = value.astype(BF16)
    return high, (value - high.astype(F32)).astype(BF16)


def dot3(lhs_hi, lhs_lo, rhs_hi, rhs_lo):
    return (
        jnp.dot(lhs_hi, rhs_hi, preferred_element_type=F32)
        + jnp.dot(lhs_lo, rhs_hi, preferred_element_type=F32)
        + jnp.dot(lhs_hi, rhs_lo, preferred_element_type=F32)
    )


def lanes_of(shape):
    return lax.broadcasted_iota(jnp.int32, shape, len(shape) - 1)


def bit_of(code, position):
    return lax.shift_right_logical(code, position) & 1


PLANE_ORDER = ((0, 1), (2, 3), (7, 6), (5, 4))


def flip_index(code):
    return lanes_of(code.shape) ^ (bit_of(code, 1) * 56 + bit_of(code, 2) * 7)


SIDE = (64, 32, 32)


def on_first_side(shape, direction):
    return (lanes_of(shape) & SIDE[direction]) == 0


def corner_of(code):
    return bit_of(code, 0) * 4 + bit_of(code, 1) * 2 + bit_of(code, 2)


def permute(value, index):
    return jnp.take_along_axis(value, index, axis=1)


def flip_in(tiles, code):
    mirrored = bit_of(code, 0) == 1
    index = flip_index(code)
    first, second = permute(tiles[0], index), permute(tiles[1], index)
    third, fourth = permute(tiles[3], index ^ 64), permute(tiles[2], index ^ 64)
    return [
        jnp.where(mirrored, third, first),
        jnp.where(mirrored, fourth, second),
        jnp.where(mirrored, first, third),
        jnp.where(mirrored, second, fourth),
    ]


def flip_out(tiles, code):
    mirrored = bit_of(code, 0) == 1
    index = flip_index(code)
    return [
        permute(jnp.where(mirrored, tiles[2], tiles[0]), index),
        permute(jnp.where(mirrored, tiles[3], tiles[1]), index),
        permute(jnp.where(mirrored, tiles[1], tiles[3]), index ^ 64),
        permute(jnp.where(mirrored, tiles[0], tiles[2]), index ^ 64),
    ]


def turn(value):
    return pltpu.roll(value, FACE // 2, 1)


def to_first(value):
    return pltpu.roll(value, 96, 1)


def to_second(value):
    return pltpu.roll(value, 32, 1)


CODE_BITS = 9
CHUNK = 16


def flip_kernel(
    last_x, x_ref, neigh_ref, orient_ref, block_ref, slope_ref,
    code_ref, un_ref, nua_ref, nda_ref, pma_ref, ppa_ref, xp_ref,
):
    group = x_ref.shape[1]
    rows = x_ref.shape[3]
    place_x, place_y = pl.program_id(0), pl.program_id(1)
    square = lax.broadcasted_iota(jnp.int32, (rows, rows), 0) == lanes_of((rows, rows))

    def flips(half):
        here_y = pl.ds(place_y * group + half, 1)
        word = orient_ref[place_x, here_y, :] + (block_ref[place_x, here_y, :] << CODE_BITS)
        for face in range(6):
            word = word + jnp.where(neigh_ref[place_x, face, here_y, :] < 0, 1 << (3 + face), 0)
        column = jnp.sum(jnp.where(square, word.astype(F32), 0.0), axis=1, keepdims=True)
        code_ref[0, half] = jnp.broadcast_to(column, (rows, FACE)).astype(jnp.int32)

        def body(step, carry):
            here = pl.ds(pl.multiple_of(step * CHUNK, CHUNK), CHUNK)
            code = code_ref[0, half, here, :]
            lower = on_first_side((CHUNK, FACE), 0)
            for field in range(FIELDS):
                parts = flip_in(
                    [
                        x_ref[0, half, field, here, FACE * tile : FACE * (tile + 1)]
                        for tile in range(4)
                    ],
                    code,
                )
                plain = parts[0] * slope_ref[0]
                cross = parts[0] * slope_ref[4]
                for tile in range(1, 4):
                    plain = plain + parts[tile] * slope_ref[tile]
                    cross = cross + parts[tile] * slope_ref[4 + tile]
                for tile in range(4):
                    un_ref[0, half, field, here, FACE * tile : FACE * (tile + 1)] = parts[tile]
                state = jnp.where(lower, parts[0], turn(parts[2]))
                slope = plain + turn(cross)
                turned = turn(state)
                nua_ref[0, half, field, here, :] = state
                nda_ref[0, half, field, here, :] = slope
                pma_ref[0, half, field, here, :] = jnp.where(lower, slope, turned)
                ppa_ref[0, half, field, here, :] = jnp.where(lower, turned, slope)
            return carry

        lax.fori_loop(0, rows // CHUNK, body, 0)

    for half in range(group):
        flips(half)

    @pl.when(place_x == last_x)
    def _():
        xp_ref[...] = ppa_ref[0]

def trace_kernel(
    x_ref, pma_ref, thi_ref, tlo_ref, nu_ref, nd_ref, pm_ref, pp_ref, ac_ref, jc_ref, ym_ref, yp_ref, xm_ref, *scratch
):
    group = x_ref.shape[1]
    rows = x_ref.shape[3]
    place_y = pl.program_id(1)
    per = len(scratch) // group

    def splits(half):
        hi_ref, lo_ref = scratch[per * half : per * half + 2]
        high, low = split(x_ref[0, half].reshape(FIELDS * rows, NODES))
        hi_ref[...] = high
        lo_ref[...] = low

    def traces(half):
        hi_ref, lo_ref, side_ref, found_ref = scratch[per * half : per * half + 4]
        for part, found in enumerate(half_traces(hi_ref, lo_ref, thi_ref, tlo_ref, 2 * FACE)):
            found_ref[part] = found

    def faces(half):
        hi_ref, lo_ref, side_ref, found_ref = scratch[per * half : per * half + 4]
        lower = lanes_of((8, FACE)) < FACE // 2
        first = on_first_side((8, FACE), 2)
        last = rows // 8 - 1
        for step in range(rows // 8):
            write_b(
                rows, step, found_ref, nu_ref.at[0, half], nd_ref.at[0, half],
                pm_ref.at[pl.ds(0, 1), half], pp_ref.at[pl.ds(0, 1), half],
            )
            here = slice(step * 8, (step + 1) * 8)
            for field in range(FIELDS):
                one = tile_of(found_ref, 0, field, rows, step, FACE)
                two = tile_of(found_ref, 1, field, rows, step, FACE)
                for kind, value in ((0, jnp.where(lower, two, one)), (1, jnp.where(lower, one, two))):
                    side_ref[3 * kind, field, here, :] = value
                    side_ref[3 * kind + 1, field, 8 + step * 8 : 16 + step * 8, :] = to_first(value)
                    side_ref[3 * kind + 2, field, 8 + step * 8 : 16 + step * 8, :] = to_second(value)
                    if step == 0:
                        side_ref[3 * kind + 2, field, 8 + rows : 9 + rows, :] = to_second(value)[0:1]
                    if step == last:
                        side_ref[3 * kind + 1, field, 7:8, :] = to_first(value)[7:8]
        for step in range(rows // 8):
            here = slice(step * 8, (step + 1) * 8)
            behind = slice(7 + step * 8, 15 + step * 8)
            ahead = slice(9 + step * 8, 17 + step * 8)
            inside, outside, slopes = [], [], []
            for field in range(FIELDS):
                inside.append(side_ref[0, field, here, :])
                outside.append(
                    jnp.where(first, side_ref[1, field, behind, :], side_ref[2, field, ahead, :])
                )
                far = jnp.where(first, side_ref[4, field, behind, :], side_ref[5, field, ahead, :])
                slopes.append(turn(far - side_ref[3, field, here, :]))
            totals, jumps = face_jumps(2, inside, outside, slopes)
            for field in range(FIELDS):
                ac_ref[0, half, field, here, :] = totals[field]
                jc_ref[0, half, field, here, :] = jumps[field]

    @pl.when(pl.program_id(0) == 0)
    def _():
        xm_ref[...] = pma_ref[0]

    splits(0)
    traces(0)
    for half in range(group):
        if half + 1 < group:
            splits(half + 1)
            traces(half + 1)
        faces(half)

    @pl.when(place_y == 0)
    def _():
        ym_ref[0] = pm_ref[0, 0]

    @pl.when(place_y == pl.num_programs(1) - 1)
    def _():
        yp_ref[0] = pp_ref[0, group - 1]


def half_traces(high, low, thi_ref, tlo_ref, width):
    half = NODES // 2
    return [
        dot3(
            high[:, half * part : half * (part + 1)],
            low[:, half * part : half * (part + 1)],
            thi_ref[half * part : half * (part + 1), :width],
            tlo_ref[half * part : half * (part + 1), :width],
        )
        for part in range(2)
    ]


def tile_of(ref, part, field, rows, step, first):
    row = field * rows + step * 8
    return ref[part, row : row + 8, first : first + FACE]


def write_b(rows, step, found_ref, nu, nd, minus_ref, plus_ref):
    here = slice(step * 8, (step + 1) * 8)
    lower = lanes_of((8, FACE)) < FACE // 2
    first = on_first_side((8, FACE), 1)
    for field in range(FIELDS):
        one = tile_of(found_ref, 0, field, rows, step, 0)
        two = tile_of(found_ref, 1, field, rows, step, 0)
        state = jnp.where(lower, one, two)
        slope = turn(jnp.where(lower, two, one))
        if nu is not None:
            nu[field, here, :] = state
            nd[field, here, :] = slope
        if minus_ref is not None:
            minus_ref[0, field, here, :] = jnp.where(first, slope, to_second(state))
        if plus_ref is not None:
            plus_ref[0, field, here, :] = jnp.where(first, to_first(state), slope)


def normal_flux(state, axis):
    density, energy = state[0], state[4]
    momentum = state[1:4]
    inverse = 1.0 / density
    kinetic = (
        momentum[0] * momentum[0] + momentum[1] * momentum[1] + momentum[2] * momentum[2]
    ) * inverse
    pressure = (HEAT_RATIO - 1.0) * (energy - 0.5 * kinetic)
    speed = momentum[axis] * inverse
    flux = [momentum[axis]]
    for part in range(3):
        value = momentum[part] * speed
        flux.append(value + pressure if part == axis else value)
    flux.append(speed * (energy + pressure))
    return flux, jnp.abs(speed) + jnp.sqrt(HEAT_RATIO * pressure * inverse)


def face_jumps(axis, inside, outside, slopes):
    flux_in, speed_in = normal_flux(inside, axis)
    flux_out, speed_out = normal_flux(outside, axis)
    wave = 0.5 * jnp.maximum(speed_in, speed_out)
    outward = jnp.where(on_first_side(inside[0].shape, axis), -0.5, 0.5)
    totals, jumps = [], []
    for field in range(FIELDS):
        jump = outside[field] - inside[field]
        change = flux_out[field] - flux_in[field] - VISCOSITY * slopes[field]
        totals.append(outward * change - wave * jump)
        jumps.append(jump)
    return totals, jumps


def volume_kernel(x_ref, mix_ref, mhi_ref, mlo_ref, v_ref, *scratch):
    group = x_ref.shape[1]
    rows = x_ref.shape[3]
    wide = NODES // 2
    per = len(scratch) // group

    def fluxes(half, step):
        hi_ref, lo_ref, part_ref = scratch[per * half : per * half + 3]
        here = slice(step * CHUNK, (step + 1) * CHUNK)

        def put(field, slot, tile, value):
            where_rows = slice(field * rows + step * CHUNK, field * rows + (step + 1) * CHUNK)
            first = wide * slot + FACE * tile
            high, low = split(value)
            hi_ref[where_rows, first : first + FACE] = high
            lo_ref[where_rows, first : first + FACE] = low

        def parity(flow):
            return (
                [flow[idx] + flow[2 + idx] for idx in range(2)],
                [flow[idx] - flow[2 + idx] for idx in range(2)],
            )

        tiles = [slice(FACE * tile, FACE * (tile + 1)) for tile in range(4)]
        derived = []
        for lanes in tiles:
            fields = [x_ref[0, half, field, here, lanes] for field in range(FIELDS)]
            density, energy = fields[0], fields[4]
            momentum = fields[1:4]
            inverse = 1.0 / density
            kinetic = (
                momentum[0] * momentum[0] + momentum[1] * momentum[1] + momentum[2] * momentum[2]
            ) * inverse
            pressure = (HEAT_RATIO - 1.0) * (energy - 0.5 * kinetic)
            derived.append((inverse, pressure))

        def flux(field, axis, tile):
            lanes = tiles[tile]
            inverse, pressure = derived[tile]
            moment = x_ref[0, half, 1 + axis, here, lanes]
            if field == 0:
                return moment
            speed = moment * inverse
            if field == 4:
                return (x_ref[0, half, 4, here, lanes] + pressure) * speed
            found = x_ref[0, half, field, here, lanes] * speed
            return found + pressure if field == 1 + axis else found

        for field in range(FIELDS):
            sources = [
                [x_ref[0, half, field, here, lanes] for lanes in tiles],
                [flux(field, 1, tile) for tile in range(4)],
                [flux(field, 2, tile) for tile in range(4)],
            ]
            for slot, flow in enumerate(sources):
                even, odd = parity(flow)
                for tile in range(2):
                    put(field, slot, tile, even[tile])
                    put(field, 3 + slot, tile, odd[tile])
            even, odd = parity([flux(field, 0, tile) for tile in range(4)])
            where_rows = slice(field * rows + step * CHUNK, field * rows + (step + 1) * CHUNK)
            for kind, flow in ((0, odd), (1, even)):
                turned = [turn(value) for value in flow]
                for first in range(2):
                    base = 8 * (1 - kind) + 4 * first
                    part_ref[kind, where_rows, FACE * first : FACE * (first + 1)] = sum(
                        flow[second] * mix_ref[base + 2 * second]
                        + turned[second] * mix_ref[base + 2 * second + 1]
                        for second in range(2)
                    )

    def products(half):
        hi_ref, lo_ref, part_ref = scratch[per * half : per * half + 3]
        for kind in range(2):
            first = 3 * wide * kind
            slots = [
                (slice(first, first + wide), slice(wide * kind, wide * (kind + 1))),
                (slice(first + wide, first + 3 * wide), slice(2 * wide, 4 * wide)),
            ]
            total = part_ref[kind]
            for lanes, block in slots:
                for lhs, rhs in ((hi_ref, mhi_ref), (lo_ref, mhi_ref), (hi_ref, mlo_ref)):
                    total = total + jnp.dot(lhs[:, lanes], rhs[block, :], preferred_element_type=F32)
                yield
            part_ref[kind] = total

    def combine(half, step):
        part_ref = scratch[per * half + 2]
        for field in range(FIELDS):
            here = slice(step * CHUNK, (step + 1) * CHUNK)
            where_rows = slice(field * rows + step * CHUNK, field * rows + (step + 1) * CHUNK)
            for first in range(2):
                lanes = slice(FACE * first, FACE * (first + 1))
                even = part_ref[0, where_rows, lanes]
                odd = part_ref[1, where_rows, lanes]
                v_ref[0, half, field, here, lanes] = even + odd
                v_ref[0, half, field, here, FACE * (2 + first) : FACE * (3 + first)] = even - odd

    chunks = rows // CHUNK
    for step in range(chunks):
        fluxes(0, step)
    for half in range(group):
        work = products(half)
        for step in range(chunks):
            next(work, None)
            if half > 0:
                combine(half - 1, step)
            if half + 1 < group:
                fluxes(half + 1, step)
        for _ in work:
            pass
    for step in range(chunks):
        combine(group - 1, step)


def face_kernel(place_x, last_x, w_end, olds, *refs):
    (
        v_ref, code_ref, lift_ref, nua_ref, nda_ref, left_ref, right_ref, nub_ref, ndb_ref, bl_ref, br_ref,
        bm_ref, bp_ref, hyl_ref, hyr_ref, ac_ref, jc_ref, lhi_ref, llo_ref, rhi_ref, rlo_ref,
    ) = refs[:21]
    final = place_x == last_x
    rest = refs[21 + (1 if olds else 0) :]
    if final:
        flat_ref, *older = rest[: 1 + olds]
        rate_ref, sums_ref, coarse_ref, *scratch = rest[1 + olds :]
    else:
        rate_ref, coarse_ref, *scratch = rest
    group = v_ref.shape[0]
    rows = v_ref.shape[2]
    place_y = pl.program_id(0)
    half_nodes = NODES // 2
    per = len(scratch) // group
    shape = (CHUNK, FACE)
    at_start = place_y == 0
    at_end = place_y == pl.num_programs(0) - 1

    def gather_faces(half):
        hi_ref, lo_ref, aj_ref = scratch[per * half : per * half + 3]
        lower = lanes_of(shape) < FACE // 2
        for step in range(rows // CHUNK):
            here = slice(step * CHUNK, (step + 1) * CHUNK)
            code = code_ref[half, here, :]
            for axis in range(2):
                first = on_first_side(shape, axis)
                wall = jnp.where(first, bit_of(code, 3 + 2 * axis), bit_of(code, 4 + 2 * axis)) == 1
                states, lefts, rights, tilts = [], [], [], []
                for field in range(FIELDS):
                    at = (field, here, slice(None))
                    if axis == 0:
                        states.append(nua_ref[half][at])
                        tilts.append(nda_ref[half][at])
                        lefts.append(left_ref[half][at])
                        rights.append(right_ref[half][at])
                    else:
                        states.append(nub_ref[half][at])
                        tilts.append(ndb_ref[half][at])
                        if half > 0:
                            lefts.append(bp_ref[half - 1][at])
                        else:
                            lefts.append(jnp.where(at_start, hyl_ref[at], bl_ref[at]))
                        if half + 1 < group:
                            rights.append(bm_ref[half + 1][at])
                        else:
                            rights.append(jnp.where(at_end, hyr_ref[at], br_ref[at]))
                if axis == 0:
                    crossed = [
                        turn(jnp.where(first, right, left)) for left, right in zip(lefts, rights)
                    ]
                else:
                    crossed = [
                        jnp.where(first, to_first(left), to_second(right))
                        for left, right in zip(lefts, rights)
                    ]
                outside, slopes = [], []
                for field in range(FIELDS):
                    far = jnp.where(first, lefts[field], rights[field])
                    mirror = -states[field] if field == 1 + axis else states[field]
                    outside.append(jnp.where(wall, mirror, far))
                    slopes.append(jnp.where(wall, 0.0, crossed[field] - tilts[field]))
                totals, jumps = face_jumps(axis, states, outside, slopes)
                for field in range(FIELDS):
                    total, jump = totals[field], jumps[field]
                    where_rows = slice(field * rows + step * CHUNK, field * rows + (step + 1) * CHUNK)
                    if axis == 0:
                        aj_ref[where_rows, :FACE] = total * (-TIME_STEP / w_end)
                        aj_ref[where_rows, FACE:] = jump
                        continue
                    total_c, jump_c = ac_ref[half, field, here, :], jc_ref[half, field, here, :]
                    for slot, value in (
                        (0, jnp.where(lower, total, total_c)),
                        (1, jnp.where(lower, jump, jump_c)),
                        (2, jnp.where(lower, total_c, total)),
                        (3, jnp.where(lower, jump_c, jump)),
                    ):
                        high, low = split(value)
                        hi_ref[where_rows, FACE * slot : FACE * (slot + 1)] = high
                        lo_ref[where_rows, FACE * slot : FACE * (slot + 1)] = low

    def apply(half):
        hi_ref, lo_ref, aj_ref = scratch[per * half : per * half + 3]
        change = []
        for side in range(2):
            lanes = slice(half_nodes * side, half_nodes * (side + 1))
            change.append(dot3(hi_ref[:, lanes], lo_ref[:, lanes], lhi_ref[lanes, :], llo_ref[lanes, :]))
        lower = lanes_of(shape) < FACE // 2
        for field in range(FIELDS):
            for step in range(rows // CHUNK):
                here = slice(step * CHUNK, (step + 1) * CHUNK)
                where_rows = slice(field * rows + step * CHUNK, field * rows + (step + 1) * CHUNK)
                total = aj_ref[where_rows, :FACE]
                jump = aj_ref[where_rows, FACE:]
                turned = turn(jump)
                top = slant = None
                values = []
                for tile in range(4):
                    lanes = slice(FACE * tile, FACE * (tile + 1))
                    inner = slice(FACE * (tile % 2), FACE * (tile % 2 + 1))
                    value = v_ref[half, field, here, lanes] + change[tile // 2][where_rows, inner]
                    value = value + jump * lift_ref[tile] + turned * lift_ref[4 + tile]
                    if tile == 0:
                        value = value + jnp.where(lower, total, 0.0)
                    if tile == 2:
                        value = value + jnp.where(lower, turn(total), 0.0)
                    values.append(value)
                    bent = value * lift_ref[8 + tile]
                    top = value if top is None else top + value
                    slant = bent if slant is None else slant + bent
                values = flip_out(values, code_ref[half, here, :])
                for tile in range(4):
                    rate_ref[half, field, here, FACE * tile : FACE * (tile + 1)] = values[tile]
                high, low = split(top)
                hi_ref[where_rows, :FACE] = high
                lo_ref[where_rows, :FACE] = low
                high, low = split(slant)
                hi_ref[where_rows, FACE : 2 * FACE] = high
                lo_ref[where_rows, FACE : 2 * FACE] = low
        coarse = dot3(hi_ref[:, : 2 * FACE], lo_ref[:, : 2 * FACE], rhi_ref[...], rlo_ref[...])
        packed = coarse[:rows]
        for field in range(1, FIELDS):
            packed = packed + pltpu.roll(coarse[field * rows : (field + 1) * rows], CORNERS * field, 1)
        lane = lanes_of((rows, 128))
        packed = jnp.where(lane == FIELDS * CORNERS, 1.0, packed)
        place = (place_y * group + half) * rows
        coarse_ref[pl.ds(pl.multiple_of(place, rows), rows), :] = packed

    gather_faces(0)
    for half in range(group):
        if half + 1 < group:
            gather_faces(half + 1)
        apply(half)

    if final:

        @pl.when(at_end)
        def _():
            height = sums_ref.shape[0]
            count = sums_ref.shape[1]
            stacked = jnp.concatenate([ref[...] for ref in older] + [coarse_ref[...]], axis=0)
            high, low = split(stacked.T[:height])
            slots = lanes_of((stacked.shape[0], count))
            block = lax.shift_right_logical(flat_ref[...], CODE_BITS)
            wide = jnp.concatenate([block] * (count // 128), axis=1)
            onehot = jnp.where(wide == slots, 1.0, 0.0).astype(BF16)
            sums_ref[...] = jnp.dot(high, onehot, preferred_element_type=F32) + jnp.dot(
                low, onehot, preferred_element_type=F32
            )


def prolong_kernel(sums_ref, more_ref, code_ref, spread_ref, out_ref, table_ref):
    group = out_ref.shape[1]
    rows = out_ref.shape[3]
    count = sums_ref.shape[1]
    width = FIELDS * CORNERS

    @pl.when((pl.program_id(0) == 0) & (pl.program_id(1) == 0))
    def _():
        total = sums_ref[...] + more_ref[...]
        scaled = total[:width] / (total[width : width + 1] + 1.0)
        high = scaled.astype(BF16).astype(F32)
        low = scaled - high
        pad = jnp.zeros((128 - 3 * width, count), F32)
        table_ref[...] = jnp.concatenate([high, low, high, pad], axis=0).astype(BF16)

    code = code_ref[0].reshape(group * rows, 128)
    slots = lanes_of((group * rows, count))
    wide = jnp.concatenate([lax.shift_right_logical(code, CODE_BITS)] * (count // 128), axis=1)
    onehot = jnp.where(wide == slots, 1.0, 0.0).astype(BF16)
    picked = lax.dot_general(
        onehot, table_ref[...], (((1,), (1,)), ((), ())), preferred_element_type=F32
    )
    picked = permute(picked, lanes_of(code.shape) ^ corner_of(code)).astype(BF16)
    for field in range(FIELDS):
        lanes = slice(NODES * field, NODES * (field + 1))
        found = jnp.dot(picked, spread_ref[:, lanes], preferred_element_type=F32)
        out_ref[0, :, field] = found.reshape(group, rows, NODES)


def whole(array):
    dims = array.ndim
    return pl.BlockSpec(array.shape, lambda *_: (0,) * dims, pipeline_mode=pl.Buffered(1))


def params(dims):
    return pltpu.CompilerParams(
        dimension_semantics=("arbitrary",) * dims, vmem_limit_bytes=VMEM_BYTES
    )


def shift(value, axis, step):
    count = lax.axis_size(axis)
    return lax.ppermute(value, axis, [(i, (i + step) % count) for i in range(count)])


def per_device(conserved, neighbours, orientation, coarse_block):
    data = tables()
    cx, cy, cz = conserved.shape[:3]
    last_x, last_y = cx - 1, cy - 1
    state = jnp.transpose(conserved, (0, 1, 3, 2, 4))
    neigh = jnp.transpose(neighbours, (0, 3, 1, 2))
    count = lax.axis_size("grp") * (cx * cy * cz // 4)
    height = 48

    def state_spec(step):
        return pl.BlockSpec((1, step, FIELDS, cz, NODES), lambda x, y: (x, y, 0, 0, 0))

    def code_spec(step):
        return pl.BlockSpec((1, step, cz, 128), lambda x, y: (x, y, 0, 0))

    def pack_spec(step):
        return pl.BlockSpec((1, step, FIELDS, cz, FACE), lambda x, y: (x, y, 0, 0, 0))

    state_shape = jax.ShapeDtypeStruct((cx, cy, FIELDS, cz, NODES), F32)
    pack_shape = jax.ShapeDtypeStruct((cx, cy, FIELDS, cz, FACE), F32)
    code_shape = jax.ShapeDtypeStruct((cx, cy, cz, 128), jnp.int32)
    consts = {
        name: [jnp.asarray(m) for m in data[name]]
        for name in ("planes", "traces", "lifts", "restrict")
    }
    lane_data = {
        name: jnp.asarray(lane_rows(rows, CHUNK)) for name, rows in data["lanes"].items()
    }

    step = 2 if cy % 2 == 0 else 1
    grid = (cx, cy // step)
    edge_x = (step, FIELDS, cz, FACE)
    edge_y = (1, FIELDS, cz, FACE)
    last_step = grid[1] - 1
    args = [state, neigh, orientation, coarse_block, lane_data["slope"]]
    code, natural, nua, nda, pma, ppa, xp = pl.pallas_call(
        functools.partial(flip_kernel, last_x),
        grid=grid,
        in_specs=[state_spec(step)] + [whole(arg) for arg in args[1:]],
        out_specs=[code_spec(step), state_spec(step)]
        + [pack_spec(step)] * 4
        + [pl.BlockSpec(edge_x, lambda x, y: (jnp.where(x == last_x, y, 0), 0, 0, 0))],
        out_shape=[code_shape, state_shape]
        + [pack_shape] * 4
        + [jax.ShapeDtypeStruct((cy, FIELDS, cz, FACE), F32)],
        compiler_params=params(2),
        name="flips",
    )(*args)
    from_left = shift(xp, "el", 1)

    step = TRACE_STEP if cy % TRACE_STEP == 0 else 1
    args = [natural, pma] + consts["traces"]
    last_step = cy // step - 1
    edge_x = (step, FIELDS, cz, FACE)
    nub, ndb, pmb, ppb, ac, jc, ym, yp, xm = pl.pallas_call(
        trace_kernel,
        grid=(cx, cy // step),
        in_specs=[
            state_spec(step),
            pl.BlockSpec(
                (1, step, FIELDS, cz, FACE), lambda x, y: (0, jnp.where(x == 0, y, last_step), 0, 0, 0)
            ),
        ]
        + [whole(arg) for arg in args[2:]],
        out_specs=[pack_spec(step)] * 6
        + [pl.BlockSpec(edge_y, lambda x, y: (x, 0, 0, 0))] * 2
        + [pl.BlockSpec(edge_x, lambda x, y: (jnp.where(x == 0, y, last_step), 0, 0, 0))],
        out_shape=[pack_shape] * 6
        + [jax.ShapeDtypeStruct((cx, FIELDS, cz, FACE), F32)] * 2
        + [jax.ShapeDtypeStruct((cy, FIELDS, cz, FACE), F32)],
        scratch_shapes=[
            pltpu.VMEM((FIELDS * cz, NODES), BF16),
            pltpu.VMEM((FIELDS * cz, NODES), BF16),
            pltpu.VMEM((6, FIELDS, cz + 16, FACE), F32),
            pltpu.VMEM((2, FIELDS * cz, 2 * FACE), F32),
        ]
        * step,
        compiler_params=params(2),
        name="traces",
    )(*args)
    from_right = shift(xm, "el", -1)
    from_below = shift(yp, "grp", 1)
    from_above = shift(ym, "grp", -1)

    step = VOLUME_STEP if cy % VOLUME_STEP == 0 else 1
    args = [natural, lane_data["mix"]] + consts["planes"]
    volume = pl.pallas_call(
        volume_kernel,
        grid=(cx, cy // step),
        in_specs=[state_spec(step)] + [whole(arg) for arg in args[1:]],
        out_specs=state_spec(step),
        out_shape=state_shape,
        scratch_shapes=[
            pltpu.VMEM((FIELDS * cz, 3 * NODES), BF16),
            pltpu.VMEM((FIELDS * cz, 3 * NODES), BF16),
            pltpu.VMEM((2, FIELDS * cz, NODES // 2), F32),
        ]
        * step,
        compiler_params=params(2),
        name="volume",
    )(*args)

    step = FACE_STEP if cy % FACE_STEP == 0 else 1
    lifts = consts["lifts"] + consts["restrict"]
    rate, olds = None, []
    for x in range(cx):
        rate, *found = face_call(
            x, cx, step, data["w_end"], rate, olds, code,
            volume, lane_data["lift"], (nua, nda), from_left if x == 0 else ppa,
            from_right if x == last_x else pma, (nub, ndb, ppb, pmb), (from_below, from_above),
            (ac, jc), lifts, (height, count),
        )
        olds = olds + found[-1:]
    sums = found[0]

    size = lax.axis_size("grp")
    more = jnp.zeros_like(sums)
    if size & (size - 1) == 0:
        stride = 1
        while stride < size:
            if stride > 1:
                sums = sums + more
            more = lax.ppermute(sums, "grp", [(i, i ^ stride) for i in range(size)])
            stride *= 2
    else:
        sums = lax.psum(sums, "grp")

    step = 2 if cy % 2 == 0 else 1
    spread = jnp.asarray(data["spread"])
    update = pl.pallas_call(
        prolong_kernel,
        grid=(cx, cy // step),
        in_specs=[whole(sums), whole(more), code_spec(step), whole(spread)],
        out_specs=state_spec(step),
        out_shape=state_shape,
        scratch_shapes=[pltpu.VMEM((128, count), BF16)],
        compiler_params=params(2),
        name="prolong",
    )(sums, more, code, spread)
    back = (0, 1, 3, 2, 4)
    return (jnp.transpose(rate, back), jnp.transpose(update, back))


def face_call(x, cx, step, w_end, rate, olds, code, volume, lift, own_a, left, right, own_b, halo_y, own_c, lifts, table):
    cy, cz = volume.shape[1], volume.shape[3]
    last_x, last_y = cx - 1, cy - 1
    final = x == last_x

    def at_x(width, place):
        return pl.BlockSpec((None, step, FIELDS, cz, width), lambda y: (place, y, 0, 0, 0))

    def beside(array, place):
        if array.ndim == 5:
            return at_x(FACE, place)
        return pl.BlockSpec((step, FIELDS, cz, FACE), lambda y: (y, 0, 0, 0))

    def single(place_of):
        return pl.BlockSpec((None, None, FIELDS, cz, FACE), lambda y: (x, place_of(y), 0, 0, 0))

    edge_y = pl.BlockSpec((None, FIELDS, cz, FACE), lambda y: (x, 0, 0, 0))
    own = at_x(FACE, x)
    nub, ndb, ppb, pmb = own_b
    args = [volume, code, lift, *own_a, left, right, nub, ndb, ppb, pmb, pmb, ppb, *halo_y, *own_c, *lifts]
    specs = [
        at_x(NODES, x),
        pl.BlockSpec((None, step, cz, 128), lambda y: (x, y, 0, 0)),
        whole(lift),
        own,
        own,
        beside(left, x - 1),
        beside(right, x + 1),
        own,
        own,
        single(lambda y: jnp.maximum(y * step - 1, 0)),
        single(lambda y: jnp.minimum(y * step + step, last_y)),
        own,
        own,
        edge_y,
        edge_y,
        own,
        own,
    ] + [whole(m) for m in lifts]
    alias = {}
    if rate is not None:
        alias = {len(args): 0}
        args.append(rate)
        specs.append(pl.BlockSpec(memory_space=pl.ANY))
    out_specs = [at_x(NODES, x)]
    out_shape = [jax.ShapeDtypeStruct((cx, cy, FIELDS, cz, NODES), F32)]
    coarse_shape = (cy * cz, 128)
    scratch = []
    if final:
        flat = code.reshape(cx * cy * cz, 128)
        args += [flat] + olds
        specs += [whole(flat)] + [whole(old) for old in olds]
        out_specs.append(pl.BlockSpec(table, lambda y: (0, 0)))
        out_shape.append(jax.ShapeDtypeStruct(table, F32))
        scratch.append(pltpu.VMEM(coarse_shape, F32))
    else:
        out_specs.append(pl.BlockSpec(coarse_shape, lambda y: (0, 0)))
        out_shape.append(jax.ShapeDtypeStruct(coarse_shape, F32))
    scratch += [
        pltpu.VMEM((FIELDS * cz, NODES), BF16),
        pltpu.VMEM((FIELDS * cz, NODES), BF16),
        pltpu.VMEM((FIELDS * cz, 2 * FACE), F32),
    ] * step
    return pl.pallas_call(
        functools.partial(face_kernel, x, last_x, w_end, len(olds)),
        grid=(cy // step,),
        in_specs=specs,
        out_specs=out_specs,
        out_shape=out_shape,
        input_output_aliases=alias,
        scratch_shapes=scratch,
        compiler_params=params(1),
        name="faces" + str(x),
    )(*args)


def solution(mesh):
    in_specs = (
        P("el", "grp", None, None, None),
        P("el", "grp", None, None),
        P("el", "grp", None),
        P("el", "grp", None),
    )
    out_specs = (P("el", "grp", None, None, None), P("el", "grp", None, None, None))
    return jax.shard_map(
        per_device, mesh=mesh, in_specs=in_specs, out_specs=out_specs, check_vma=False
    )
```

```python
import functools
import jax
import jax.numpy as jnp
import numpy as np
from jax import lax
from jax.experimental import pallas as pl
from jax.experimental.pallas import tpu as pltpu
from jax.sharding import PartitionSpec as P

NP = 8
NODES = NP**3
FACE = 2 * NP * NP
ITERS = 4
FIELDS = 5
CORNERS = 8

HEAT_RATIO = 1.4
VISCOSITY = 0.02
TIME_STEP = 0.01
COARSE_SHIFT = 1.0
RELAX = 2.0 / 3.0

F32 = jnp.float32
BF16 = jnp.bfloat16
VMEM_BYTES = 58 * 1024 * 1024
VOLUME_STEP = 2
FACE_STEP = 2
TRACE_STEP = 4
FLIP_STEP = 2
PROLONG_STEP = 4


def legendre_rows(points, degree):
    rows = [points * 0.0 + 1.0, points.copy()]
    for order in range(1, degree):
        rows.append(
            ((2 * order + 1) * points * rows[order] - order * rows[order - 1]) / (order + 1)
        )
    return rows


def node_tables(npoints):
    degree = npoints - 1
    points = np.cos(np.pi * np.arange(npoints) / degree)
    for sweep_idx in range(100):
        values = legendre_rows(points, degree)
        previous = points
        points = previous - (previous * values[degree] - values[degree - 1]) / (
            npoints * values[degree]
        )
    points = np.sort(points)
    legendre = legendre_rows(points, degree)[degree]
    weights = 2.0 / (degree * (degree + 1) * legendre**2)
    derivative = np.zeros((npoints, npoints))
    for row_idx in range(npoints):
        for col_idx in range(npoints):
            if row_idx != col_idx:
                derivative[row_idx, col_idx] = (
                    legendre[row_idx] / legendre[col_idx] / (points[row_idx] - points[col_idx])
                )
    derivative[0, 0] = -degree * (degree + 1) / 4.0
    derivative[-1, -1] = degree * (degree + 1) / 4.0
    linear = np.stack([(1.0 - points) / 2.0, (1.0 + points) / 2.0], axis=1)
    return (weights, derivative, linear)


def hi_lo(matrix):
    high = np.asarray(matrix, np.float32).astype(jnp.bfloat16)
    rest = np.asarray(matrix, np.float64) - high.astype(np.float64)
    return high, rest.astype(np.float32).astype(jnp.bfloat16)


@functools.lru_cache(maxsize=None)
def tables():
    weights, der, linear = node_tables(NP)
    w_end = weights[0]
    eye = np.eye(NP)
    full = [
        np.kron(np.kron(der, eye), eye),
        np.kron(np.kron(eye, der), eye),
        np.kron(np.kron(eye, eye), der),
    ]
    out = {"w_end": w_end, "derivative": der}
    lap = sum(mat @ mat for mat in full)
    half = NODES // 2
    mirror = np.arange(NODES).reshape(NP, NP * NP)[::-1].reshape(-1)
    lap = TIME_STEP * VISCOSITY * lap
    lap_even = 0.5 * (lap[:half, :half] + lap[:half, mirror[:half]])
    lap_odd = 0.5 * (lap[:half, :half] - lap[:half, mirror[:half]])
    flows = [-0.5 * TIME_STEP * full[axis].T[:half, :half] for axis in (1, 2)]
    out["planes"] = hi_lo(np.concatenate([lap_even.T, lap_odd.T] + flows, axis=0))
    node = np.arange(half)
    coords = [node // (NP * NP), node // NP % NP, node % NP]
    traces, lifts = [], []
    for half_idx in range(2):
        blocks, lift_rows = [], []
        for direction in (1, 2):
            other = coords[3 - direction]
            sel = np.zeros((half, FACE // 2))
            own = np.zeros((FACE // 2, half))
            ext = np.zeros((FACE // 2, half))
            for side in range(2):
                end = side * (NP - 1)
                lane = side * 32 + coords[0] * NP + other
                on_face = coords[direction] == end
                sel[node[on_face], lane[on_face]] = 1.0
                own[lane[on_face], node[on_face]] = -TIME_STEP / w_end
                ext[lane, node] = (
                    TIME_STEP * VISCOSITY * (2 * side - 1) / (2.0 * w_end) * der[coords[direction], end]
                )
            slope = full[direction].T[:half, :half] @ sel
            blocks += [sel, slope] if half_idx == direction - 1 else [slope, sel]
            lift_rows.append((own, ext))
        traces.append(np.concatenate(blocks, axis=1))
        if half_idx == 1:
            lift_rows = lift_rows[::-1]
        lifts.append(
            np.concatenate([row[0] for row in lift_rows] + [row[1] for row in lift_rows], axis=0)
        )
    out["traces"] = hi_lo(np.concatenate(traces, axis=0))
    out["lifts"] = hi_lo(np.concatenate(lifts, axis=0))
    lane = np.arange(FACE)
    upper = lane // (FACE // 2)
    pos_b, pos_c = lane // NP % NP, lane % NP
    restrict = np.zeros((2 * FACE, 128))
    for idx in range(CORNERS):
        weight = 0.5 / TIME_STEP * linear[pos_b, idx // 2 % 2] * linear[pos_c, idx % 2]
        restrict[:FACE, idx] = weight
        restrict[FACE:, idx] = weight * (2 * (idx // 4) - 1)
    out["restrict"] = hi_lo(restrict)
    place = linear[:, 1] - linear[:, 0]
    planes = [np.where(upper == 1, second, first) for first, second in PLANE_ORDER]
    rows = [place[plane] for plane in planes]
    flow = -TIME_STEP * der
    even = 0.5 * (flow[:4, :4] + flow[:4, :3:-1])
    odd = 0.5 * (flow[:4, :4] - flow[:4, :3:-1])
    mix = []
    for part in (even, odd):
        for first in range(2):
            for second in range(2):
                mix.append(part[2 * first + upper, 2 * second + upper])
                mix.append(part[2 * first + upper, 2 * second + 1 - upper])
    ends = (NP - 1) * upper
    slope_plain = [der[ends, plane] for plane in planes]
    slope_cross = [der[NP - 1 - ends, plane] for plane in planes]
    scale = TIME_STEP * VISCOSITY / (2.0 * w_end)
    lift_plain = [scale * (2 * upper - 1) * der[plane, ends] for plane in planes]
    lift_cross = [scale * (1 - 2 * upper) * der[plane, NP - 1 - ends] for plane in planes]
    out["lanes"] = {
        "mix": mix,
        "slope": slope_plain + slope_cross,
        "lift": lift_plain + lift_cross + rows,
    }
    adjacency = np.zeros((CORNERS, CORNERS))
    for idx in range(CORNERS):
        for bit in range(3):
            adjacency[idx, idx ^ (1 << bit)] = 1.0
    diagonal = COARSE_SHIFT + 3.0
    operator = diagonal * np.eye(CORNERS) - adjacency
    smooth = np.zeros((CORNERS, CORNERS))
    for sweep_idx in range(ITERS):
        smooth = smooth + RELAX * (np.eye(CORNERS) - operator @ smooth) / diagonal
    node = np.arange(NODES)
    coords = [node // (NP * NP), node // NP % NP, node % NP]
    corner = np.zeros((NODES, CORNERS))
    for idx in range(CORNERS):
        corner[:, idx] = (
            linear[coords[0], idx // 4] * linear[coords[1], idx // 2 % 2] * linear[coords[2], idx % 2]
        )
    prolong = TIME_STEP * corner @ smooth
    width = FIELDS * CORNERS
    spread = np.zeros((width, FIELDS * NODES))
    for field in range(FIELDS):
        spread[
            field * CORNERS : (field + 1) * CORNERS, field * NODES : (field + 1) * NODES
        ] = prolong.T
    spread_hi, spread_lo = hi_lo(spread)
    out["spread"] = np.concatenate(
        [spread_hi, spread_hi, spread_lo, np.zeros((128 - 3 * width, FIELDS * NODES), spread_hi.dtype)],
        axis=0,
    )
    return out


def lane_rows(rows, height):
    return np.stack([np.broadcast_to(row, (height, FACE)) for row in rows]).astype(np.float32)


def split(value):
    high = value.astype(BF16)
    return high, (value - high.astype(F32)).astype(BF16)


def dot3(lhs_hi, lhs_lo, rhs_hi, rhs_lo):
    return (
        jnp.dot(lhs_hi, rhs_hi, preferred_element_type=F32)
        + jnp.dot(lhs_lo, rhs_hi, preferred_element_type=F32)
        + jnp.dot(lhs_hi, rhs_lo, preferred_element_type=F32)
    )


def lanes_of(shape):
    return lax.broadcasted_iota(jnp.int32, shape, len(shape) - 1)


def bit_of(code, position):
    return lax.shift_right_logical(code, position) & 1


PLANE_ORDER = ((0, 1), (2, 3), (7, 6), (5, 4))


def flip_index(code):
    return lanes_of(code.shape) ^ (bit_of(code, 1) * 56 + bit_of(code, 2) * 7)


SIDE = (64, 32, 32)


def on_first_side(shape, direction):
    return (lanes_of(shape) & SIDE[direction]) == 0


def corner_of(code):
    return bit_of(code, 0) * 4 + bit_of(code, 1) * 2 + bit_of(code, 2)


def permute(value, index):
    return jnp.take_along_axis(value, index, axis=1)


def flip_in(tiles, code):
    mirrored = bit_of(code, 0) == 1
    index = flip_index(code)
    first, second = permute(tiles[0], index), permute(tiles[1], index)
    third, fourth = permute(tiles[3], index ^ 64), permute(tiles[2], index ^ 64)
    return [
        jnp.where(mirrored, third, first),
        jnp.where(mirrored, fourth, second),
        jnp.where(mirrored, first, third),
        jnp.where(mirrored, second, fourth),
    ]


def flip_out(tiles, code):
    mirrored = bit_of(code, 0) == 1
    index = flip_index(code)
    return [
        permute(jnp.where(mirrored, tiles[2], tiles[0]), index),
        permute(jnp.where(mirrored, tiles[3], tiles[1]), index),
        permute(jnp.where(mirrored, tiles[1], tiles[3]), index ^ 64),
        permute(jnp.where(mirrored, tiles[0], tiles[2]), index ^ 64),
    ]


def turn(value):
    return pltpu.roll(value, FACE // 2, 1)


def to_first(value):
    return pltpu.roll(value, 96, 1)


def to_second(value):
    return pltpu.roll(value, 32, 1)


CODE_BITS = 9
CHUNK = 16


def flip_kernel(place_x, *refs):
    x_ref, neigh_ref, orient_ref, block_ref, slope_ref = refs[:5]
    code_ref, un_ref, pma_ref, ppa_ref, *edge = refs[-5:] if len(refs) == 10 else refs[-4:]
    group = x_ref.shape[1]
    rows = x_ref.shape[3]
    place_y = pl.program_id(0)
    square = lax.broadcasted_iota(jnp.int32, (rows, rows), 0) == lanes_of((rows, rows))

    def flips(half):
        here_y = pl.ds(place_y * group + half, 1)
        word = orient_ref[place_x, here_y, :] + (block_ref[place_x, here_y, :] << CODE_BITS)
        for face in range(6):
            word = word + jnp.where(neigh_ref[place_x, face, here_y, :] < 0, 1 << (3 + face), 0)
        column = jnp.sum(jnp.where(square, word.astype(F32), 0.0), axis=1, keepdims=True)
        code_ref[0, half] = jnp.broadcast_to(column, (rows, FACE)).astype(jnp.int32)

        def body(step, carry):
            here = pl.ds(pl.multiple_of(step * CHUNK, CHUNK), CHUNK)
            code = code_ref[0, half, here, :]
            lower = on_first_side((CHUNK, FACE), 0)
            for field in range(FIELDS):
                parts = flip_in(
                    [
                        x_ref[0, half, field, here, FACE * tile : FACE * (tile + 1)]
                        for tile in range(4)
                    ],
                    code,
                )
                plain = parts[0] * slope_ref[0]
                cross = parts[0] * slope_ref[4]
                for tile in range(1, 4):
                    plain = plain + parts[tile] * slope_ref[tile]
                    cross = cross + parts[tile] * slope_ref[4 + tile]
                for tile in range(4):
                    un_ref[0, half, field, here, FACE * tile : FACE * (tile + 1)] = parts[tile]
                state = jnp.where(lower, parts[0], turn(parts[2]))
                slope = plain + turn(cross)
                turned = turn(state)
                pma_ref[0, half, field, here, :] = jnp.where(lower, slope, turned)
                ppa_ref[0, half, field, here, :] = jnp.where(lower, turned, slope)
            return carry

        lax.fori_loop(0, rows // CHUNK, body, 0, unroll=2)

    for half in range(group):
        flips(half)
    if edge:
        edge[0][...] = ppa_ref[0]


def trace_kernel(
    x_ref, pma_ref, thi_ref, tlo_ref, pm_ref, pp_ref, ac_ref, jc_ref, ym_ref, yp_ref, xm_ref, *scratch
):
    group = x_ref.shape[1]
    rows = x_ref.shape[3]
    place_y = pl.program_id(1)
    per = len(scratch) // group

    def splits(half):
        hi_ref, lo_ref = scratch[per * half : per * half + 2]
        high, low = split(x_ref[0, half].reshape(FIELDS * rows, NODES))
        hi_ref[...] = high
        lo_ref[...] = low

    def traces(half):
        hi_ref, lo_ref, side_ref, found_ref = scratch[per * half : per * half + 4]
        for part, found in enumerate(half_traces(hi_ref, lo_ref, thi_ref, tlo_ref, 2 * FACE)):
            found_ref[part] = found

    def faces(half):
        hi_ref, lo_ref, side_ref, found_ref = scratch[per * half : per * half + 4]
        lower = lanes_of((8, FACE)) < FACE // 2
        first = on_first_side((8, FACE), 2)
        last = rows // 8 - 1
        for step in range(rows // 8):
            write_b(rows, step, found_ref, pm_ref.at[0, half], pp_ref.at[0, half])
            here = slice(step * 8, (step + 1) * 8)
            for field in range(FIELDS):
                one = tile_of(found_ref, 0, field, rows, step, FACE)
                two = tile_of(found_ref, 1, field, rows, step, FACE)
                for kind, value in ((0, jnp.where(lower, two, one)), (1, jnp.where(lower, one, two))):
                    side_ref[3 * kind, field, here, :] = value
                    side_ref[3 * kind + 1, field, 8 + step * 8 : 16 + step * 8, :] = to_first(value)
                    side_ref[3 * kind + 2, field, 8 + step * 8 : 16 + step * 8, :] = to_second(value)
                    if step == 0:
                        side_ref[3 * kind + 2, field, 8 + rows : 9 + rows, :] = to_second(value)[0:1]
                    if step == last:
                        side_ref[3 * kind + 1, field, 7:8, :] = to_first(value)[7:8]
        for step in range(rows // 8):
            here = slice(step * 8, (step + 1) * 8)
            behind = slice(7 + step * 8, 15 + step * 8)
            ahead = slice(9 + step * 8, 17 + step * 8)
            inside, outside, slopes = [], [], []
            for field in range(FIELDS):
                inside.append(side_ref[0, field, here, :])
                outside.append(
                    jnp.where(first, side_ref[1, field, behind, :], side_ref[2, field, ahead, :])
                )
                far = jnp.where(first, side_ref[4, field, behind, :], side_ref[5, field, ahead, :])
                slopes.append(turn(far - side_ref[3, field, here, :]))
            totals, jumps = face_jumps(2, inside, outside, slopes)
            for field in range(FIELDS):
                ac_ref[0, half, field, here, :] = totals[field]
                jc_ref[0, half, field, here, :] = jumps[field]

    @pl.when(pl.program_id(0) == 0)
    def _():
        xm_ref[...] = pma_ref[0]

    splits(0)
    traces(0)
    for half in range(group):
        if half + 1 < group:
            splits(half + 1)
            traces(half + 1)
        faces(half)

    @pl.when(place_y == 0)
    def _():
        ym_ref[0] = pm_ref[0, 0]

    @pl.when(place_y == pl.num_programs(1) - 1)
    def _():
        yp_ref[0] = pp_ref[0, group - 1]


def half_traces(high, low, thi_ref, tlo_ref, width):
    half = NODES // 2
    return [
        dot3(
            high[:, half * part : half * (part + 1)],
            low[:, half * part : half * (part + 1)],
            thi_ref[half * part : half * (part + 1), :width],
            tlo_ref[half * part : half * (part + 1), :width],
        )
        for part in range(2)
    ]


def tile_of(ref, part, field, rows, step, first):
    row = field * rows + step * 8
    return ref[part, row : row + 8, first : first + FACE]


def write_b(rows, step, found_ref, minus_ref, plus_ref):
    here = slice(step * 8, (step + 1) * 8)
    lower = lanes_of((8, FACE)) < FACE // 2
    first = on_first_side((8, FACE), 1)
    for field in range(FIELDS):
        one = tile_of(found_ref, 0, field, rows, step, 0)
        two = tile_of(found_ref, 1, field, rows, step, 0)
        state = jnp.where(lower, one, two)
        slope = jnp.where(lower, two, one)
        minus_ref[field, here, :] = jnp.where(first, slope, to_second(state))
        plus_ref[field, here, :] = jnp.where(first, to_first(state), slope)


def normal_flux(state, axis):
    density, energy = state[0], state[4]
    momentum = state[1:4]
    inverse = 1.0 / density
    kinetic = (
        momentum[0] * momentum[0] + momentum[1] * momentum[1] + momentum[2] * momentum[2]
    ) * inverse
    pressure = (HEAT_RATIO - 1.0) * (energy - 0.5 * kinetic)
    speed = momentum[axis] * inverse
    flux = [momentum[axis]]
    for part in range(3):
        value = momentum[part] * speed
        flux.append(value + pressure if part == axis else value)
    flux.append(speed * (energy + pressure))
    return flux, jnp.abs(speed) + jnp.sqrt(HEAT_RATIO * pressure * inverse)


def face_jumps(axis, inside, outside, slopes):
    flux_in, speed_in = normal_flux(inside, axis)
    flux_out, speed_out = normal_flux(outside, axis)
    wave = 0.5 * jnp.maximum(speed_in, speed_out)
    outward = jnp.where(on_first_side(inside[0].shape, axis), -0.5, 0.5)
    totals, jumps = [], []
    for field in range(FIELDS):
        jump = outside[field] - inside[field]
        change = flux_out[field] - flux_in[field] - VISCOSITY * slopes[field]
        totals.append(outward * change - wave * jump)
        jumps.append(jump)
    return totals, jumps


def volume_kernel(x_ref, mix_ref, mhi_ref, mlo_ref, v_ref, *scratch):
    group = x_ref.shape[1]
    rows = x_ref.shape[3]
    wide = NODES // 2
    per = len(scratch) // group

    def fluxes(half, step):
        hi_ref, lo_ref, part_ref = scratch[per * half : per * half + 3]
        here = slice(step * CHUNK, (step + 1) * CHUNK)

        def put(field, slot, tile, value):
            where_rows = slice(field * rows + step * CHUNK, field * rows + (step + 1) * CHUNK)
            first = wide * slot + FACE * tile
            high, low = split(value)
            hi_ref[where_rows, first : first + FACE] = high
            lo_ref[where_rows, first : first + FACE] = low

        def parity(flow):
            return (
                [flow[idx] + flow[2 + idx] for idx in range(2)],
                [flow[idx] - flow[2 + idx] for idx in range(2)],
            )

        tiles = [slice(FACE * tile, FACE * (tile + 1)) for tile in range(4)]
        derived = []
        for lanes in tiles:
            fields = [x_ref[0, half, field, here, lanes] for field in range(FIELDS)]
            density, energy = fields[0], fields[4]
            momentum = fields[1:4]
            inverse = 1.0 / density
            kinetic = (
                momentum[0] * momentum[0] + momentum[1] * momentum[1] + momentum[2] * momentum[2]
            ) * inverse
            pressure = (HEAT_RATIO - 1.0) * (energy - 0.5 * kinetic)
            derived.append((inverse, pressure))

        def flux(field, axis, tile):
            lanes = tiles[tile]
            inverse, pressure = derived[tile]
            moment = x_ref[0, half, 1 + axis, here, lanes]
            if field == 0:
                return moment
            speed = moment * inverse
            if field == 4:
                return (x_ref[0, half, 4, here, lanes] + pressure) * speed
            found = x_ref[0, half, field, here, lanes] * speed
            return found + pressure if field == 1 + axis else found

        for field in range(FIELDS):
            sources = [
                [x_ref[0, half, field, here, lanes] for lanes in tiles],
                [flux(field, 1, tile) for tile in range(4)],
                [flux(field, 2, tile) for tile in range(4)],
            ]
            for slot, flow in enumerate(sources):
                even, odd = parity(flow)
                for tile in range(2):
                    put(field, slot, tile, even[tile])
                    put(field, 3 + slot, tile, odd[tile])
            even, odd = parity([flux(field, 0, tile) for tile in range(4)])
            where_rows = slice(field * rows + step * CHUNK, field * rows + (step + 1) * CHUNK)
            for kind, flow in ((0, odd), (1, even)):
                turned = [turn(value) for value in flow]
                for first in range(2):
                    base = 8 * (1 - kind) + 4 * first
                    part_ref[kind, where_rows, FACE * first : FACE * (first + 1)] = sum(
                        flow[second] * mix_ref[base + 2 * second]
                        + turned[second] * mix_ref[base + 2 * second + 1]
                        for second in range(2)
                    )

    def products(half):
        hi_ref, lo_ref, part_ref = scratch[per * half : per * half + 3]
        for kind in range(2):
            first = 3 * wide * kind
            slots = [
                (slice(first, first + wide), slice(wide * kind, wide * (kind + 1))),
                (slice(first + wide, first + 3 * wide), slice(2 * wide, 4 * wide)),
            ]
            total = part_ref[kind]
            for lanes, block in slots:
                for lhs, rhs in ((hi_ref, mhi_ref), (lo_ref, mhi_ref), (hi_ref, mlo_ref)):
                    total = total + jnp.dot(lhs[:, lanes], rhs[block, :], preferred_element_type=F32)
                yield
            part_ref[kind] = total

    def combine(half, step):
        part_ref = scratch[per * half + 2]
        for field in range(FIELDS):
            here = slice(step * CHUNK, (step + 1) * CHUNK)
            where_rows = slice(field * rows + step * CHUNK, field * rows + (step + 1) * CHUNK)
            for first in range(2):
                lanes = slice(FACE * first, FACE * (first + 1))
                even = part_ref[0, where_rows, lanes]
                odd = part_ref[1, where_rows, lanes]
                v_ref[0, half, field, here, lanes] = even + odd
                v_ref[0, half, field, here, FACE * (2 + first) : FACE * (3 + first)] = even - odd

    chunks = rows // CHUNK
    for step in range(chunks):
        fluxes(0, step)
    for half in range(group):
        work = products(half)
        for step in range(chunks):
            next(work, None)
            if half > 0:
                combine(half - 1, step)
            if half + 1 < group:
                fluxes(half + 1, step)
        for _ in work:
            pass
    for step in range(chunks):
        combine(group - 1, step)


def face_kernel(place_x, last_x, w_end, olds, *refs):
    (
        v_ref, code_ref, lift_ref, am_ref, ap_ref, left_ref, right_ref, bl_ref, br_ref,
        bm_ref, bp_ref, hyl_ref, hyr_ref, ac_ref, jc_ref, lhi_ref, llo_ref, rhi_ref, rlo_ref,
    ) = refs[:19]
    final = place_x == last_x
    rest = refs[19 + (1 if olds else 0) :]
    if final:
        flat_ref, *older = rest[: 1 + olds]
        rate_ref, sums_ref, coarse_ref, *scratch = rest[1 + olds :]
    else:
        rate_ref, coarse_ref, *scratch = rest
    group = v_ref.shape[0]
    rows = v_ref.shape[2]
    place_y = pl.program_id(0)
    half_nodes = NODES // 2
    per = len(scratch) // group
    shape = (CHUNK, FACE)
    at_start = place_y == 0
    at_end = place_y == pl.num_programs(0) - 1

    def gather_faces(half):
        hi_ref, lo_ref, aj_ref = scratch[per * half : per * half + 3]
        lower = lanes_of(shape) < FACE // 2
        for step in range(rows // CHUNK):
            here = slice(step * CHUNK, (step + 1) * CHUNK)
            code = code_ref[half, here, :]
            for axis in range(2):
                first = on_first_side(shape, axis)
                wall = jnp.where(first, bit_of(code, 3 + 2 * axis), bit_of(code, 4 + 2 * axis)) == 1
                states, lefts, rights, tilts = [], [], [], []
                for field in range(FIELDS):
                    at = (field, here, slice(None))
                    if axis == 0:
                        minus, plus = am_ref[half][at], ap_ref[half][at]
                        states.append(turn(jnp.where(first, plus, minus)))
                        tilts.append(jnp.where(first, minus, plus))
                        lefts.append(left_ref[half][at])
                        rights.append(right_ref[half][at])
                    else:
                        minus, plus = bm_ref[half][at], bp_ref[half][at]
                        states.append(jnp.where(first, to_first(minus), to_second(plus)))
                        tilts.append(jnp.where(first, minus, plus))
                        if half > 0:
                            lefts.append(bp_ref[half - 1][at])
                        else:
                            lefts.append(jnp.where(at_start, hyl_ref[at], bl_ref[at]))
                        if half + 1 < group:
                            rights.append(bm_ref[half + 1][at])
                        else:
                            rights.append(jnp.where(at_end, hyr_ref[at], br_ref[at]))
                if axis == 0:
                    crossed = [
                        turn(jnp.where(first, right, left)) for left, right in zip(lefts, rights)
                    ]
                else:
                    crossed = [
                        jnp.where(first, to_first(left), to_second(right))
                        for left, right in zip(lefts, rights)
                    ]
                outside, slopes = [], []
                for field in range(FIELDS):
                    far = jnp.where(first, lefts[field], rights[field])
                    mirror = -states[field] if field == 1 + axis else states[field]
                    outside.append(jnp.where(wall, mirror, far))
                    slope = crossed[field] - tilts[field]
                    slopes.append(jnp.where(wall, 0.0, turn(slope) if axis else slope))
                totals, jumps = face_jumps(axis, states, outside, slopes)
                for field in range(FIELDS):
                    total, jump = totals[field], jumps[field]
                    where_rows = slice(field * rows + step * CHUNK, field * rows + (step + 1) * CHUNK)
                    if axis == 0:
                        aj_ref[where_rows, :FACE] = total * (-TIME_STEP / w_end)
                        aj_ref[where_rows, FACE:] = jump
                        continue
                    total_c, jump_c = ac_ref[half, field, here, :], jc_ref[half, field, here, :]
                    for slot, value in (
                        (0, jnp.where(lower, total, total_c)),
                        (1, jnp.where(lower, jump, jump_c)),
                        (2, jnp.where(lower, total_c, total)),
                        (3, jnp.where(lower, jump_c, jump)),
                    ):
                        high, low = split(value)
                        hi_ref[where_rows, FACE * slot : FACE * (slot + 1)] = high
                        lo_ref[where_rows, FACE * slot : FACE * (slot + 1)] = low

    def apply(half):
        hi_ref, lo_ref, aj_ref = scratch[per * half : per * half + 3]
        change = []
        for side in range(2):
            lanes = slice(half_nodes * side, half_nodes * (side + 1))
            change.append(dot3(hi_ref[:, lanes], lo_ref[:, lanes], lhi_ref[lanes, :], llo_ref[lanes, :]))
        lower = lanes_of(shape) < FACE // 2
        for field in range(FIELDS):
            for step in range(rows // CHUNK):
                here = slice(step * CHUNK, (step + 1) * CHUNK)
                where_rows = slice(field * rows + step * CHUNK, field * rows + (step + 1) * CHUNK)
                total = aj_ref[where_rows, :FACE]
                jump = aj_ref[where_rows, FACE:]
                turned = turn(jump)
                top = slant = None
                values = []
                for tile in range(4):
                    lanes = slice(FACE * tile, FACE * (tile + 1))
                    inner = slice(FACE * (tile % 2), FACE * (tile % 2 + 1))
                    value = v_ref[half, field, here, lanes] + change[tile // 2][where_rows, inner]
                    value = value + jump * lift_ref[tile] + turned * lift_ref[4 + tile]
                    if tile == 0:
                        value = value + jnp.where(lower, total, 0.0)
                    if tile == 2:
                        value = value + jnp.where(lower, turn(total), 0.0)
                    values.append(value)
                    bent = value * lift_ref[8 + tile]
                    top = value if top is None else top + value
                    slant = bent if slant is None else slant + bent
                values = flip_out(values, code_ref[half, here, :])
                for tile in range(4):
                    rate_ref[half, field, here, FACE * tile : FACE * (tile + 1)] = values[tile]
                high, low = split(top)
                hi_ref[where_rows, :FACE] = high
                lo_ref[where_rows, :FACE] = low
                high, low = split(slant)
                hi_ref[where_rows, FACE : 2 * FACE] = high
                lo_ref[where_rows, FACE : 2 * FACE] = low
        coarse = dot3(hi_ref[:, : 2 * FACE], lo_ref[:, : 2 * FACE], rhi_ref[...], rlo_ref[...])
        packed = coarse[:rows]
        for field in range(1, FIELDS):
            packed = packed + pltpu.roll(coarse[field * rows : (field + 1) * rows], CORNERS * field, 1)
        lane = lanes_of((rows, 128))
        packed = jnp.where(lane == FIELDS * CORNERS, 1.0, packed)
        place = (place_y * group + half) * rows
        coarse_ref[pl.ds(pl.multiple_of(place, rows), rows), :] = packed

    gather_faces(0)
    for half in range(group):
        if half + 1 < group:
            gather_faces(half + 1)
        apply(half)

    if final:

        @pl.when(at_end)
        def _():
            height = sums_ref.shape[0]
            count = sums_ref.shape[1]
            stacked = jnp.concatenate([ref[...] for ref in older] + [coarse_ref[...]], axis=0)
            high, low = split(stacked.T[:height])
            slots = lanes_of((stacked.shape[0], count))
            block = lax.shift_right_logical(flat_ref[...], CODE_BITS)
            wide = jnp.concatenate([block] * (count // 128), axis=1)
            onehot = jnp.where(wide == slots, 1.0, 0.0).astype(BF16)
            sums_ref[...] = jnp.dot(high, onehot, preferred_element_type=F32) + jnp.dot(
                low, onehot, preferred_element_type=F32
            )


def prolong_kernel(sums_ref, more_ref, code_ref, spread_ref, out_ref, table_ref):
    group = out_ref.shape[1]
    rows = out_ref.shape[3]
    count = sums_ref.shape[1]
    width = FIELDS * CORNERS

    @pl.when((pl.program_id(0) == 0) & (pl.program_id(1) == 0))
    def _():
        total = sums_ref[...] + more_ref[...]
        scaled = total[:width] / (total[width : width + 1] + 1.0)
        high = scaled.astype(BF16).astype(F32)
        low = scaled - high
        pad = jnp.zeros((128 - 3 * width, count), F32)
        table_ref[...] = jnp.concatenate([high, low, high, pad], axis=0).astype(BF16)

    code = code_ref[0].reshape(group * rows, 128)
    slots = lanes_of((group * rows, count))
    wide = jnp.concatenate([lax.shift_right_logical(code, CODE_BITS)] * (count // 128), axis=1)
    onehot = jnp.where(wide == slots, 1.0, 0.0).astype(BF16)
    picked = lax.dot_general(
        onehot, table_ref[...], (((1,), (1,)), ((), ())), preferred_element_type=F32
    )
    picked = permute(picked, lanes_of(code.shape) ^ corner_of(code)).astype(BF16)
    for field in range(FIELDS):
        lanes = slice(NODES * field, NODES * (field + 1))
        found = jnp.dot(picked, spread_ref[:, lanes], preferred_element_type=F32)
        out_ref[0, :, field] = found.reshape(group, rows, NODES)


def whole(array):
    dims = array.ndim
    return pl.BlockSpec(array.shape, lambda *_: (0,) * dims, pipeline_mode=pl.Buffered(1))


def params(dims):
    return pltpu.CompilerParams(
        dimension_semantics=("arbitrary",) * dims, vmem_limit_bytes=VMEM_BYTES
    )


def shift(value, axis, step):
    count = lax.axis_size(axis)
    return lax.ppermute(value, axis, [(i, (i + step) % count) for i in range(count)])


def per_device(conserved, neighbours, orientation, coarse_block):
    data = tables()
    cx, cy, cz = conserved.shape[:3]
    last_x, last_y = cx - 1, cy - 1
    state = jnp.transpose(conserved, (0, 1, 3, 2, 4))
    neigh = jnp.transpose(neighbours, (0, 3, 1, 2))
    count = lax.axis_size("grp") * (cx * cy * cz // 4)
    height = 48

    def state_spec(step):
        return pl.BlockSpec((1, step, FIELDS, cz, NODES), lambda x, y: (x, y, 0, 0, 0))

    def code_spec(step):
        return pl.BlockSpec((1, step, cz, 128), lambda x, y: (x, y, 0, 0))

    def pack_spec(step):
        return pl.BlockSpec((1, step, FIELDS, cz, FACE), lambda x, y: (x, y, 0, 0, 0))

    state_shape = jax.ShapeDtypeStruct((cx, cy, FIELDS, cz, NODES), F32)
    pack_shape = jax.ShapeDtypeStruct((cx, cy, FIELDS, cz, FACE), F32)
    code_shape = jax.ShapeDtypeStruct((cx, cy, cz, 128), jnp.int32)
    consts = {
        name: [jnp.asarray(m) for m in data[name]]
        for name in ("planes", "traces", "lifts", "restrict")
    }
    lane_data = {
        name: jnp.asarray(lane_rows(rows, CHUNK)) for name, rows in data["lanes"].items()
    }

    step = FLIP_STEP if cy % FLIP_STEP == 0 else 1
    grid = (cx, cy // step)
    edge_x = (step, FIELDS, cz, FACE)
    edge_y = (1, FIELDS, cz, FACE)
    last_step = grid[1] - 1
    found = []
    for x in [last_x] + list(range(last_x)):
        found = flip_call(x, step, state, neigh, orientation, coarse_block, lane_data["slope"], found)
        if x == last_x:
            xp = found[-1]
        found = found[:4]
    code, natural, pma, ppa = found
    from_left = shift(xp, "el", 1)

    step = TRACE_STEP if cy % TRACE_STEP == 0 else 1
    args = [natural, pma] + consts["traces"]
    last_step = cy // step - 1
    edge_x = (step, FIELDS, cz, FACE)
    pmb, ppb, ac, jc, ym, yp, xm = pl.pallas_call(
        trace_kernel,
        grid=(cx, cy // step),
        in_specs=[
            state_spec(step),
            pl.BlockSpec(
                (1, step, FIELDS, cz, FACE), lambda x, y: (0, jnp.where(x == 0, y, last_step), 0, 0, 0)
            ),
        ]
        + [whole(arg) for arg in args[2:]],
        out_specs=[pack_spec(step)] * 4
        + [pl.BlockSpec(edge_y, lambda x, y: (x, 0, 0, 0))] * 2
        + [pl.BlockSpec(edge_x, lambda x, y: (jnp.where(x == 0, y, last_step), 0, 0, 0))],
        out_shape=[pack_shape] * 4
        + [jax.ShapeDtypeStruct((cx, FIELDS, cz, FACE), F32)] * 2
        + [jax.ShapeDtypeStruct((cy, FIELDS, cz, FACE), F32)],
        scratch_shapes=[
            pltpu.VMEM((FIELDS * cz, NODES), BF16),
            pltpu.VMEM((FIELDS * cz, NODES), BF16),
            pltpu.VMEM((6, FIELDS, cz + 16, FACE), F32),
            pltpu.VMEM((2, FIELDS * cz, 2 * FACE), F32),
        ]
        * step,
        compiler_params=params(2),
        name="traces",
    )(*args)
    from_right = shift(xm, "el", -1)
    from_below = shift(yp, "grp", 1)
    from_above = shift(ym, "grp", -1)

    step = VOLUME_STEP if cy % VOLUME_STEP == 0 else 1
    args = [natural, lane_data["mix"]] + consts["planes"]
    volume = pl.pallas_call(
        volume_kernel,
        grid=(cx, cy // step),
        in_specs=[state_spec(step)] + [whole(arg) for arg in args[1:]],
        out_specs=state_spec(step),
        out_shape=state_shape,
        scratch_shapes=[
            pltpu.VMEM((FIELDS * cz, 3 * NODES), BF16),
            pltpu.VMEM((FIELDS * cz, 3 * NODES), BF16),
            pltpu.VMEM((2, FIELDS * cz, NODES // 2), F32),
        ]
        * step,
        compiler_params=params(2),
        name="volume",
    )(*args)

    step = FACE_STEP if cy % FACE_STEP == 0 else 1
    lifts = consts["lifts"] + consts["restrict"]
    rate, olds = None, []
    for x in range(cx):
        rate, *found = face_call(
            x, cx, step, data["w_end"], rate, olds, code,
            volume, lane_data["lift"], (pma, ppa), from_left if x == 0 else ppa,
            from_right if x == last_x else pma, (ppb, pmb), (from_below, from_above),
            (ac, jc), lifts, (height, count),
        )
        olds = olds + found[-1:]
    sums = found[0]

    size = lax.axis_size("grp")
    more = jnp.zeros_like(sums)
    if size & (size - 1) == 0:
        stride = 1
        while stride < size:
            if stride > 1:
                sums = sums + more
            more = lax.ppermute(sums, "grp", [(i, i ^ stride) for i in range(size)])
            stride *= 2
    else:
        sums = lax.psum(sums, "grp")

    step = PROLONG_STEP if cy % PROLONG_STEP == 0 else 1
    spread = jnp.asarray(data["spread"])
    update = pl.pallas_call(
        prolong_kernel,
        grid=(cx, cy // step),
        in_specs=[whole(sums), whole(more), code_spec(step), whole(spread)],
        out_specs=state_spec(step),
        out_shape=state_shape,
        scratch_shapes=[pltpu.VMEM((128, count), BF16)],
        compiler_params=params(2),
        name="prolong",
    )(sums, more, code, spread)
    back = (0, 1, 3, 2, 4)
    return (jnp.transpose(rate, back), jnp.transpose(update, back))


def flip_call(x, step, state, neigh, orient, block, slope, found):
    cx, cy, _, cz = state.shape[:4]
    first = not found

    def at_x(*block):
        zeros = (0,) * (len(block) - 2)
        return pl.BlockSpec(block, lambda y: (x, y) + zeros)

    args = [state, neigh, orient, block, slope] + list(found)
    pack = (1, step, FIELDS, cz, FACE)
    out_specs = [at_x(1, step, cz, 128), at_x(1, step, FIELDS, cz, NODES), at_x(*pack), at_x(*pack)]
    shapes = [((cx, cy, cz, 128), jnp.int32), (state.shape, F32)]
    shapes += [((cx, cy, FIELDS, cz, FACE), F32)] * 2
    if first:
        out_specs.append(pl.BlockSpec(pack[1:], lambda y: (y, 0, 0, 0)))
        shapes.append(((cy, FIELDS, cz, FACE), F32))
    return pl.pallas_call(
        functools.partial(flip_kernel, x),
        grid=(cy // step,),
        in_specs=[at_x(1, step, FIELDS, cz, NODES)]
        + [whole(arg) for arg in args[1:5]]
        + [pl.BlockSpec(memory_space=pl.ANY)] * len(found),
        out_specs=out_specs,
        out_shape=[jax.ShapeDtypeStruct(*shape) for shape in shapes],
        input_output_aliases={5 + idx: idx for idx in range(len(found))},
        compiler_params=params(1),
        name="flips" + str(x),
    )(*args)


def face_call(x, cx, step, w_end, rate, olds, code, volume, lift, own_a, left, right, own_b, halo_y, own_c, lifts, table):
    cy, cz = volume.shape[1], volume.shape[3]
    last_x, last_y = cx - 1, cy - 1
    final = x == last_x

    def at_x(width, place):
        return pl.BlockSpec((None, step, FIELDS, cz, width), lambda y: (place, y, 0, 0, 0))

    def beside(array, place):
        if array.ndim == 5:
            return at_x(FACE, place)
        return pl.BlockSpec((step, FIELDS, cz, FACE), lambda y: (y, 0, 0, 0))

    def single(place_of):
        return pl.BlockSpec((None, None, FIELDS, cz, FACE), lambda y: (x, place_of(y), 0, 0, 0))

    edge_y = pl.BlockSpec((None, FIELDS, cz, FACE), lambda y: (x, 0, 0, 0))
    own = at_x(FACE, x)
    ppb, pmb = own_b
    args = [volume, code, lift, *own_a, left, right, ppb, pmb, pmb, ppb, *halo_y, *own_c, *lifts]
    specs = [
        at_x(NODES, x),
        pl.BlockSpec((None, step, cz, 128), lambda y: (x, y, 0, 0)),
        whole(lift),
        own,
        own,
        beside(left, x - 1),
        beside(right, x + 1),
        single(lambda y: jnp.maximum(y * step - 1, 0)),
        single(lambda y: jnp.minimum(y * step + step, last_y)),
        own,
        own,
        edge_y,
        edge_y,
        own,
        own,
    ] + [whole(m) for m in lifts]
    alias = {}
    if rate is not None:
        alias = {len(args): 0}
        args.append(rate)
        specs.append(pl.BlockSpec(memory_space=pl.ANY))
    out_specs = [at_x(NODES, x)]
    out_shape = [jax.ShapeDtypeStruct((cx, cy, FIELDS, cz, NODES), F32)]
    coarse_shape = (cy * cz, 128)
    scratch = []
    if final:
        flat = code.reshape(cx * cy * cz, 128)
        args += [flat] + olds
        specs += [whole(flat)] + [whole(old) for old in olds]
        out_specs.append(pl.BlockSpec(table, lambda y: (0, 0)))
        out_shape.append(jax.ShapeDtypeStruct(table, F32))
        scratch.append(pltpu.VMEM(coarse_shape, F32))
    else:
        out_specs.append(pl.BlockSpec(coarse_shape, lambda y: (0, 0)))
        out_shape.append(jax.ShapeDtypeStruct(coarse_shape, F32))
    scratch += [
        pltpu.VMEM((FIELDS * cz, NODES), BF16),
        pltpu.VMEM((FIELDS * cz, NODES), BF16),
        pltpu.VMEM((FIELDS * cz, 2 * FACE), F32),
    ] * step
    return pl.pallas_call(
        functools.partial(face_kernel, x, last_x, w_end, len(olds)),
        grid=(cy // step,),
        in_specs=specs,
        out_specs=out_specs,
        out_shape=out_shape,
        input_output_aliases=alias,
        scratch_shapes=scratch,
        compiler_params=params(1),
        name="faces" + str(x),
    )(*args)


def solution(mesh):
    in_specs = (
        P("el", "grp", None, None, None),
        P("el", "grp", None, None),
        P("el", "grp", None),
        P("el", "grp", None),
    )
    out_specs = (P("el", "grp", None, None, None), P("el", "grp", None, None, None))
    return jax.shard_map(
        per_device, mesh=mesh, in_specs=in_specs, out_specs=out_specs, check_vma=False
    )
```
